32 devices in a mesh: slab: 8 (over z, y), walk: 4 (over x, core).
Axes of the slice: x: 2, y: 2, z: 4, core: 2. Of those that a mesh axis runs over, the one named last changes fastest.
Arguments:
- bias_grid: float32 [32, 512, 512], P('slab', 'walk'), may hold values from 0 to 12, as said below
- hill_slab: int32 [64, 64, 1], P(('slab', 'walk')), may hold values from 0 to 7; in each aligned block of 128 rows (0 to 127, 128 to 255, ..., all dimensions but the last counted through in order) at most 64 rows name the same one
- hill_row: int32 [64, 64], P(('slab', 'walk')), may hold values from 0 to 3
- hill_col: int32 [64, 64], P(('slab', 'walk')), may hold values from 0 to 511
- hill_depth: int32 [64, 64], P(('slab', 'walk')), may hold values from 0 to 511
- hill_level: int32 [64, 64], P(('slab', 'walk')), may hold values from 0 to 7
- hill_count: int32 [64], P(('slab', 'walk')), may hold values from 1 to 64
- height_levels: float32 [8], replicated, may hold values from 0.5 to 2
Outputs:
- new_bias: float32 [32, 512, 512], P('slab', 'walk')
- free_energy: float32 [32, 512, 512], P('slab', 'walk')
The draws below stay inside these ranges and needn't reach their ends.
Inputs may be any that keep to these rules, and one draw needn't show every extreme that they name: `bias_grid`: the bias is not negative. `hill_slab`: among the hills of one device's walkers (128 hills in a row of the flattened walkers and hills), no slab is named more than 64 times, and in some such blocks one slab is named exactly 64 times.
All inputs are finite; a program needn't handle non-finite values.
Results may differ from the reference program's by a relative error of at most 0.000082.
Values sent between devices are 32-bit elements; how exact they have to be, the bound alone decides.
A program may use at most 64 MiB of HBM per device.

```python
import math
import jax
import jax.numpy as jnp
import numpy as np
from jax import lax

ROWS_DEV = 4
DEPTH = 512
HILLS = 64
WALKERS_DEV = 2
LEVELS = 8
REACH = 8
CAP = 64
GRID_ROWS = 32
GRID_COLS = 512
WALKERS = 64
N_SLAB = 8


def draw_bias_grid(key, part):
    rough_key = jax.random.fold_in(key, 11)
    row_key = jax.random.fold_in(key, 12)
    col_key = jax.random.fold_in(key, 13)
    depth_key = jax.random.fold_in(key, 14)
    rough_cells = jax.random.uniform(rough_key, (GRID_ROWS, GRID_COLS, DEPTH), jnp.float32)
    row_scale = jnp.exp(jax.random.uniform(row_key, (GRID_ROWS, 1, 1), jnp.float32, math.log(0.5), math.log(4.0)))
    col_scale = jnp.exp(jax.random.uniform(col_key, (1, GRID_COLS, 1), jnp.float32, math.log(0.8), math.log(2.0)))
    depth_scale = jnp.exp(jax.random.uniform(depth_key, (1, 1, DEPTH), jnp.float32, math.log(0.8), math.log(1.25)))
    rough_part = rough_cells * row_scale * col_scale * depth_scale
    return rough_part


def with_ends(values, stream_key, low, top_value):
    longest = values.shape.index(max(values.shape))
    spots = []
    for shift in (0, 1):
        where = [jax.random.randint(jax.random.fold_in(stream_key, axis), (), 0, length) for axis, length in enumerate(values.shape)]
        where[longest] = (where[longest] + shift) % values.shape[longest]
        spots.append(tuple(where))
    return values.at[spots[0]].set(low).at[spots[1]].set(top_value)


def shared_out(own_key, own, number, rows, number_of, top, bound, slope):
    sequence = jax.random.permutation(own_key, number_of)
    heavy_load, usual = shares(number_of, rows * top, bound, slope, True), shares(number_of, rows * top, bound, slope, False)
    places = jnp.arange(number_of)

    def named(sizes, offset_by):
        used = int((sizes > 0).sum())
        fixed = max(1, used // 4)
        moved = fixed + (places - fixed + offset_by * (used - fixed)) % max(1, number_of - fixed)
        return jnp.zeros((number_of,), jnp.int32).at[sequence[jnp.where(places < fixed, places, moved)]].set(jnp.asarray(sizes, jnp.int32))

    sizes = jnp.where(number % 4 == 0, named(heavy_load, number // 4), named(usual, number - number // 4 - 1))
    mixed = jax.random.permutation(jax.random.fold_in(own, 3), number_of)
    source_of, taker = mixed[0:number_of // 2 * 2:2], mixed[1:number_of // 2 * 2:2]
    slack = jnp.minimum(sizes[source_of] - 1, bound - sizes[taker]) // 2
    slack = jnp.where((source_of == sequence[0]) | (taker == sequence[0]) | (sizes[taker] == 0), 0, jnp.maximum(slack, 0))
    moved = jax.random.randint(jax.random.fold_in(own, 4), (number_of // 2,), 0, 1 << 20) % (slack + 1)
    sizes = sizes.at[source_of].add(-moved).at[taker].add(moved)
    members = jnp.searchsorted(jnp.cumsum(sizes), jnp.arange(rows * top), side="right").astype(jnp.int32)
    table = members.reshape(top, rows).T
    table = table[jax.random.permutation(jax.random.fold_in(own, 1), rows)]
    offset_by = jax.random.randint(jax.random.fold_in(own, 2), (rows, 1), 0, top)
    return jnp.take_along_axis(table, (jnp.arange(top)[None, :] + offset_by) % top, axis=1)


def shares(count, total, bound, skew, full):
    portions = [(1 << 20) // math.isqrt(rank ** skew) + 1 for rank in range(1, count + 1)]
    largest = bound if full else min(bound, max(-(-total // count), total * portions[0] // sum(portions)))
    least = 1 if total - largest >= count - 1 else 0
    counts, surplus = [largest] + [least] * (count - 1), total - largest - least * (count - 1)
    while surplus > 0:
        free = [i for i in range(1, count) if counts[i] < largest] or [i for i in range(1, count) if counts[i] < bound]
        whole, budget = sum([portions[i] for i in free]), surplus
        for i in free:
            extra = min(bound - counts[i], max(1, budget * portions[i] // whole), surplus)
            counts[i] = counts[i] + extra
            surplus = surplus - extra
    return np.array(counts)


def setup_inputs(seed: int = 0) -> dict:
    streams_of = jax.random.split(jax.random.key(seed), 9)
    bias_grid = draw_bias_grid(jax.random.fold_in(streams_of[8], 71), 0)
    hill_slab_keys = jax.random.split(jax.random.fold_in(streams_of[1], 1), WALKERS * HILLS // (WALKERS_DEV * HILLS))
    hill_slab_turns = jax.random.permutation(jax.random.fold_in(streams_of[1], 3), WALKERS * HILLS // (WALKERS_DEV * HILLS))
    hill_slab = jax.vmap(lambda own, number: shared_out(jax.random.fold_in(streams_of[1], 2), own, number, WALKERS_DEV * HILLS, N_SLAB, 1, CAP, 2))(hill_slab_keys, hill_slab_turns).reshape((WALKERS, HILLS, 1))
    hill_row = with_ends(jax.random.randint(streams_of[2], (WALKERS, HILLS), 0, ROWS_DEV), jax.random.fold_in(streams_of[2], 1), 0, ROWS_DEV - 1).astype(jnp.int32)
    hill_col = with_ends(jax.random.randint(streams_of[3], (WALKERS, HILLS), 0, GRID_COLS), jax.random.fold_in(streams_of[3], 1), 0, GRID_COLS - 1).astype(jnp.int32)
    hill_depth = with_ends(jax.random.randint(streams_of[4], (WALKERS, HILLS), 0, DEPTH), jax.random.fold_in(streams_of[4], 1), 0, DEPTH - 1).astype(jnp.int32)
    hill_level = with_ends(jax.random.randint(streams_of[5], (WALKERS, HILLS), 0, LEVELS), jax.random.fold_in(streams_of[5], 1), 0, LEVELS - 1).astype(jnp.int32)
    hill_count = with_ends(jax.random.randint(streams_of[6], (WALKERS,), 1, HILLS + 1), jax.random.fold_in(streams_of[6], 1), 1, HILLS).astype(jnp.int32)
    height_levels = jnp.clip(jnp.exp(jax.random.uniform(streams_of[7], (LEVELS,), jnp.float32, math.log(0.5), math.log(2.0))), 0.5, 2.0)
    return dict(bias_grid=bias_grid, hill_slab=hill_slab, hill_row=hill_row, hill_col=hill_col, hill_depth=hill_depth, hill_level=hill_level, hill_count=hill_count, height_levels=height_levels)


BASE_HEIGHT = 1.2
TEMPER = 4.0
SIGMA_SHARE = 0.3125
FREE_SCALE = 10.0 / 9.0


def fold_axis(padded, radius, extent, axis):
    inner = lax.slice_in_dim(padded, radius, radius + extent, axis=axis)
    low_part = lax.slice_in_dim(padded, 0, radius, axis=axis)
    high_part = lax.slice_in_dim(padded, radius + extent, 2 * radius + extent, axis=axis)
    head = lax.slice_in_dim(inner, 0, radius, axis=axis) + high_part
    middle = lax.slice_in_dim(inner, radius, extent - radius, axis=axis)
    tail = lax.slice_in_dim(inner, extent - radius, extent, axis=axis) + low_part
    return jnp.concatenate([head, middle, tail], axis=axis)


def reference(bias_grid, hill_slab, hill_row, hill_col, hill_depth, hill_level, hill_count, height_levels):
    grid_rows, grid_cols, grid_depth = bias_grid.shape
    radius = REACH
    centre_row = (hill_slab[:, :, 0] * ROWS_DEV + hill_row).reshape(-1).astype(jnp.int32)
    centre_col = hill_col.reshape(-1).astype(jnp.int32)
    centre_depth = hill_depth.reshape(-1).astype(jnp.int32)
    is_live = (jnp.arange(HILLS, dtype=jnp.int32)[None, :] < hill_count[:, None]).reshape(-1)
    level_match = hill_level.reshape(-1)[:, None] == jnp.arange(LEVELS, dtype=jnp.int32)[None, :]
    base_height = jnp.sum(jnp.where(level_match, height_levels[None, :], 0.0), axis=1)
    base_height = jnp.where(is_live, BASE_HEIGHT * base_height, 0.0)
    height = base_height * jnp.exp(-bias_grid[centre_row, centre_col, centre_depth] / TEMPER)
    spread = SIGMA_SHARE * radius
    distance = (jnp.arange(2 * radius, dtype=jnp.int32) - radius).astype(jnp.float32)
    profile = jnp.exp(-(distance * distance) / (2.0 * spread * spread))

    def add_hill(padded, hill):
        weight, row_at, col_at, depth_at = hill
        patch = (weight * profile)[:, None, None] * profile[None, :, None] * profile[None, None, :]
        current = lax.dynamic_slice(padded, (row_at, col_at, depth_at), (2 * radius, 2 * radius, 2 * radius))
        return lax.dynamic_update_slice(padded, current + patch, (row_at, col_at, depth_at)), None

    start = jnp.zeros((grid_rows + 2 * radius, grid_cols + 2 * radius, grid_depth + 2 * radius), jnp.float32)
    padded, unused = lax.scan(add_hill, start, (height, centre_row, centre_col, centre_depth))
    folded = fold_axis(padded, radius, grid_rows, 0)
    folded = fold_axis(folded, radius, grid_cols, 1)
    deposit = fold_axis(folded, radius, grid_depth, 2)
    new_bias = bias_grid + deposit
    highest = jnp.max(new_bias)
    free_energy = FREE_SCALE * (highest - new_bias)
    return new_bias, free_energy
```

```python
import functools
import math

import jax
import jax.numpy as jnp
from jax import lax
from jax.experimental import pallas as pl
from jax.experimental.pallas import tpu as pltpu
from jax.sharding import PartitionSpec as P

BASE_HEIGHT = 1.2
TEMPER = 4.0
SIGMA_SHARE = 0.3125
FREE_SCALE = 10.0 / 9.0


def from_behind(block, axis, distance):
    devices = range(lax.axis_size(axis))
    route = [((i - distance) % len(devices), i) for i in devices]
    return lax.ppermute(block, axis, route)


def gaussian(position, centre, extent, radius):
    offset = jnp.mod(position - centre + extent // 2, extent) - extent // 2
    inside = (offset >= -radius) & (offset < radius)
    spread = SIGMA_SHARE * radius
    distance = offset.astype(jnp.float32)
    return jnp.where(inside, jnp.exp(-(distance * distance) / (2.0 * spread * spread)), 0.0)


def deposit(row_ids, col_ids, depth_ids, hill_lists, grid_rows, grid_cols, grid_depth, radius):
    slot_total = hill_lists.shape[1]
    block_size = math.gcd(slot_total, 256)
    row_count = row_ids.shape[0]
    col_count = col_ids.shape[0]
    depth_count = depth_ids.shape[0]

    def one_block(carry_sum, index):
        portion = lax.dynamic_slice_in_dim(hill_lists, index * block_size, block_size, 1)
        row_gauss = (
            gaussian(row_ids[:, None], portion[1].astype(jnp.int32)[None, :], grid_rows, radius)
            * portion[0][None, :]
        )
        col_gauss = gaussian(
            col_ids[:, None], portion[2].astype(jnp.int32)[None, :], grid_cols, radius
        )
        depth_gauss = gaussian(
            depth_ids[None, :], portion[3].astype(jnp.int32)[:, None], grid_depth, radius
        )
        plane_gauss = (row_gauss[:, None, :] * col_gauss[None, :, :]).reshape(
            row_count * col_count, block_size
        )
        added = jnp.dot(
            plane_gauss,
            depth_gauss,
            precision=lax.Precision.HIGHEST,
            preferred_element_type=jnp.float32,
        )
        return (carry_sum + added, None)

    start = jnp.zeros((row_count * col_count, depth_count), jnp.float32)
    result, unused = lax.scan(one_block, start, jnp.arange(slot_total // block_size))
    return result.reshape(row_count, col_count, depth_count)


def by_collectives(
    bias_grid, hill_slab, hill_row, hill_col, hill_depth, hill_level, hill_count, height_levels
):
    rows_dev, cols_dev, depth_bins = bias_grid.shape
    slab_count = lax.axis_size("slab")
    walk_count = lax.axis_size("walk")
    radius = 2 * rows_dev
    grid_rows = rows_dev * slab_count
    grid_cols = cols_dev * walk_count
    walkers_dev, hill_slots = hill_row.shape
    sent_rows = walkers_dev * hill_slots
    capacity = max(2, 4 * sent_rows // slab_count)
    target = hill_slab[:, :, 0].reshape(-1)
    centre_row = target * rows_dev + hill_row.reshape(-1)
    is_live = (
        lax.broadcasted_iota(jnp.int32, (walkers_dev, hill_slots), 1) < hill_count[:, None]
    ).reshape(-1)
    level_match = hill_level.reshape(-1)[:, None] == lax.broadcasted_iota(
        jnp.int32, (1, height_levels.shape[0]), 1
    )
    base_height = jnp.sum(jnp.where(level_match, height_levels[None, :], 0.0), axis=1)
    base_height = jnp.where(is_live, BASE_HEIGHT * base_height, 0.0)
    same_slab = target[:, None] == target[None, :]
    earlier = lax.broadcasted_iota(jnp.int32, (sent_rows, sent_rows), 1) < lax.broadcasted_iota(
        jnp.int32, (sent_rows, sent_rows), 0
    )
    slot_rank = jnp.sum((same_slab & earlier).astype(jnp.int32), axis=1)
    slot_place = target * capacity + slot_rank
    placing = (
        slot_place[:, None] == lax.broadcasted_iota(jnp.int32, (1, slab_count * capacity), 1)
    ).astype(jnp.float32)
    fields = jnp.stack(
        [
            base_height,
            centre_row.astype(jnp.float32),
            hill_col.reshape(-1).astype(jnp.float32),
            hill_depth.reshape(-1).astype(jnp.float32),
        ]
    )
    outgoing = jnp.dot(
        fields, placing, precision=lax.Precision.HIGHEST, preferred_element_type=jnp.float32
    )
    outgoing = outgoing.reshape(4, slab_count, capacity)
    arrived = lax.all_to_all(outgoing, "slab", split_axis=1, concat_axis=1, tiled=True).reshape(
        4, slab_count * capacity
    )
    shared = lax.all_gather(arrived, "walk", axis=1, tiled=True)
    slab_index = lax.axis_index("slab")
    walk_index = lax.axis_index("walk")
    local_row = jnp.clip(shared[1].astype(jnp.int32) - slab_index * rows_dev, 0, rows_dev - 1)
    local_col = shared[2].astype(jnp.int32) - walk_index * cols_dev
    local_depth = jnp.clip(shared[3].astype(jnp.int32), 0, depth_bins - 1)
    owned = (local_col >= 0) & (local_col < cols_dev)
    flat_place = (
        local_row * cols_dev + jnp.clip(local_col, 0, cols_dev - 1)
    ) * depth_bins + local_depth
    picked = bias_grid.reshape(-1)[flat_place]
    centre_value = lax.psum(jnp.where(owned, picked, 0.0), "walk")
    height = shared[0] * jnp.exp(-centre_value / TEMPER)
    hill_lists = jnp.stack([height, shared[1], shared[2], shared[3]])
    col_ids = walk_index * cols_dev + lax.broadcasted_iota(jnp.int32, (cols_dev,), 0)
    depth_ids = lax.broadcasted_iota(jnp.int32, (depth_bins,), 0)
    collected = [hill_lists]
    for offset in (-2, -1, 1, 2):
        collected.append(from_behind(hill_lists, "slab", offset))
    row_ids = slab_index * rows_dev + lax.broadcasted_iota(jnp.int32, (rows_dev,), 0)
    added = deposit(
        row_ids,
        col_ids,
        depth_ids,
        jnp.concatenate(collected, axis=1),
        grid_rows,
        grid_cols,
        depth_bins,
        radius,
    )
    new_bias = bias_grid + added
    highest = lax.pmax(jnp.max(new_bias), ("slab", "walk"))
    free_energy = FREE_SCALE * (highest - new_bias)
    return (new_bias, free_energy)


LANES = 128
F32 = jnp.float32
BF16 = jnp.bfloat16
MESH = pl.DeviceIdType.MESH
NT = (((1,), (1,)), ((), ()))


def wrapped(offset, extent):
    offset = jnp.where(offset >= extent // 2, offset - extent, offset)
    return jnp.where(offset < -(extent // 2), offset + extent, offset)


def profile(offset, radius):
    spread = SIGMA_SHARE * radius
    value = jnp.exp(-(offset * offset) / (2.0 * spread * spread))
    return jnp.where((offset >= -radius) & (offset < radius), value, 0.0)


def halves(value):
    high = value.astype(BF16)
    return high, (value - high.astype(F32)).astype(BF16)


def iota(shape, dim):
    return lax.broadcasted_iota(jnp.int32, shape, dim).astype(F32)


def window_kernel(
    slabs, walks, rows, cols, levels, per_group,
    bias_ref, slab_ref, row_ref, col_ref, depth_ref, level_ref, count_ref, table_ref,
    new_ref, top_ref,
    mine, hills, bias_high, bias_low, own, picked, tables, chosen,
    left_high, left_low, right_high, right_low, near, peak, peaks,
    a_send, a_recv, b_send, b_recv, c_send, c_recv,
):
    devices = slabs * walks
    groups = devices // per_group
    share = LANES // per_group
    cells, depth = bias_ref.shape
    radius = 2 * rows
    grid_rows, grid_cols = slabs * rows, walks * cols
    slab = lax.axis_index("slab")
    walk = lax.axis_index("walk")
    me = slab * walks + walk
    first_row = (slab * rows).astype(F32)
    first_col = (walk * cols).astype(F32)

    def place(step):
        other = lax.rem(me + step, devices)
        return (other // walks, lax.rem(other, walks))

    barrier = pltpu.get_barrier_semaphore()
    for step in range(1, devices):
        pl.semaphore_signal(barrier, inc=1, device_id=place(step), device_id_type=MESH)

    def in_row(ref):
        value = ref[...].astype(F32)
        return jnp.concatenate([value[i : i + 1] for i in range(value.shape[0])], axis=1)

    slots = row_ref.shape[1]
    lane = iota((1, LANES), 1)
    live = jnp.zeros((1, LANES), F32)
    for i in range(row_ref.shape[0]):
        inside = (lane >= i * slots) & (lane < i * slots + count_ref[i].astype(F32))
        live = jnp.where(inside, 1.0, live)
    target = in_row(slab_ref)
    centre_row = target * rows + in_row(row_ref)
    centre_col = in_row(col_ref)
    centre_depth = in_row(depth_ref)
    owner = target * walks + jnp.floor(centre_col / cols)
    owner = jnp.where(live > 0, owner, -1.0)
    owners = jnp.broadcast_to(owner, (LANES, LANES))
    same = (owners == owners.T) & (iota((LANES, LANES), 0) < iota((LANES, LANES), 1))
    rank = jnp.sum(jnp.where(same, 1.0, 0.0), axis=0, keepdims=True)
    over = jnp.max(jnp.where((live > 0) & (rank >= share), 1.0, 0.0))
    spot = rank + (lax.rem(me, per_group) * share).astype(F32)
    spot = jnp.where((live > 0) & (rank < share), spot, -1.0)
    col_high = jnp.floor(centre_col / 16.0)
    depth_high = jnp.floor(centre_depth / 16.0)
    fields = (
        jnp.where(live > 0, in_row(level_ref) + 1.0, 0.0),
        centre_row,
        col_high,
        centre_col - 16.0 * col_high,
        depth_high,
        centre_depth - 16.0 * depth_high,
        spot,
        live,
    )
    for i, field in enumerate(fields):
        mine[i : i + 1, :] = field
    hills[me] = mine[...]

    pl.semaphore_wait(barrier, devices - 1)
    a_copies = [
        pltpu.make_async_remote_copy(
            mine, hills.at[me], a_send.at[step], a_recv.at[step],
            device_id=place(step), device_id_type=MESH,
        )
        for step in range(1, devices)
    ]
    for copy in a_copies:
        copy.start()

    high, low = halves(bias_ref[...])
    bias_high[...] = high
    bias_low[...] = low
    earlier = jnp.where(
        iota((LANES, LANES), 0) < iota((LANES, LANES), 1), 1.0, 0.0
    ).astype(BF16)
    one, two = (
        lax.broadcasted_iota(jnp.int32, (devices, devices), 0),
        lax.broadcasted_iota(jnp.int32, (devices, devices), 1),
    )
    before = jnp.where((one // per_group == two // per_group) & (two < one), 1.0, 0.0).astype(BF16)

    for copy in a_copies:
        copy.wait_recv()

    there = hills[:, 7, :] > 0
    hill_row = hills[:, 1, :]
    hill_col = hills[:, 2, :] * 16.0 + hills[:, 3, :]
    away_row = hill_row - first_row
    away_col = hill_col - first_col
    owned = there & (away_row >= 0) & (away_row < rows) & (away_col >= 0) & (away_col < cols)
    own_place = jnp.where(owned, hills[:, 6, :], -1.0)

    def past(away, extent, limit):
        away = away + (radius - 1)
        away = jnp.where(away < 0, away + extent, away)
        away = jnp.where(away >= extent, away - extent, away)
        return away < limit

    close = (
        there
        & past(away_row, grid_rows, rows + 2 * radius - 1)
        & past(away_col, grid_cols, cols + 2 * radius - 1)
    )
    close_one = jnp.where(close, 1.0, 0.0)
    close_half = close_one.astype(BF16)
    rank_in = jnp.dot(close_half, earlier, preferred_element_type=F32)
    rank_of = jnp.sum(
        jnp.dot(before, close_half, preferred_element_type=F32), axis=1, keepdims=True
    )
    close_place = jnp.where(close, rank_in + rank_of, -1.0)
    over = jnp.maximum(over, jnp.max(jnp.where(close_place >= LANES, 1.0, 0.0)))

    slot = iota((LANES, per_group * LANES), 0)

    def group_fields(group):
        parts = [hills[group * per_group + i] for i in range(per_group)]
        return jnp.concatenate(parts, axis=1).astype(BF16)

    def group_places(places, group):
        parts = [
            places[group * per_group + i : group * per_group + i + 1, :] for i in range(per_group)
        ]
        matches = slot == jnp.concatenate(parts, axis=1)
        return jnp.where(matches, 1.0, 0.0).astype(BF16)

    for group in range(groups):
        own[group] = lax.dot_general(
            group_fields(group), group_places(own_place, group), NT, preferred_element_type=F32
        )

    cell_id = iota((cells, LANES), 0)
    depth_id = iota((depth, LANES), 0)

    def pick(group, carry):
        part = own[group]
        wanted = part[4:5] * 16.0 + part[5:6]
        select = jnp.where(depth_id == wanted, 1.0, 0.0).astype(BF16)
        lines = jnp.dot(bias_high[...], select, preferred_element_type=F32)
        lines = lines + jnp.dot(bias_low[...], select, preferred_element_type=F32)
        cell = (part[1:2] - first_row) * cols + part[2:3] * 16.0 + part[3:4] - first_col
        value = jnp.sum(jnp.where(cell_id == cell, lines, 0.0), axis=0, keepdims=True)
        picked[pl.ds(group, 1), :] = value
        return carry

    lax.fori_loop(0, groups, pick, 0, unroll=groups <= 8)

    offsets = [(i, j) for i in (-2, -1, 0, 1, 2) for j in (-1, 0, 1)]
    b_copies = []
    for n, (i, j) in enumerate(offsets):
        if (i, j) == (0, 0):
            continue
        device = (lax.rem(slab - i + slabs, slabs), lax.rem(walk - j + walks, walks))
        b_copies.append(
            pltpu.make_async_remote_copy(
                picked, tables.at[n], b_send.at[n], b_recv.at[n],
                device_id=device, device_id_type=MESH,
            )
        )
    for copy in b_copies:
        copy.start()

    depth_lane = iota((LANES, depth), 1)
    col_id = iota((cols, LANES), 0)
    for group in range(groups):
        data, places = group_fields(group), group_places(close_place, group)
        chosen[group] = lax.dot_general(data, places, NT, preferred_element_type=F32)
        column = lax.dot_general(places, data, NT, preferred_element_type=F32)
        at = column[:, 4:5] * 16.0 + column[:, 5:6]
        high, low = halves(profile(wrapped(depth_lane - at, depth), radius))
        right_high[group * LANES : (group + 1) * LANES, :] = high
        right_low[group * LANES : (group + 1) * LANES, :] = low
        part = chosen[group]
        at = part[2:3] * 16.0 + part[3:4]
        near[:, group * LANES : (group + 1) * LANES] = profile(
            wrapped(col_id + first_col - at, grid_cols), radius
        )

    level = chosen[:, 0, :]
    base = jnp.zeros((groups, LANES), F32)
    for i in range(levels):
        base = jnp.where(level == i + 1, BASE_HEIGHT * table_ref[i], base)
    at_row = chosen[:, 1, :]
    at_col = chosen[:, 2, :] * 16.0 + chosen[:, 3, :]
    at_spot = chosen[:, 6, :].astype(jnp.int32)
    slab_of = jnp.floor(at_row / rows) - slab.astype(F32)
    walk_of = jnp.floor(at_col / cols) - walk.astype(F32)
    slab_of = jnp.where(slab_of < -2, slab_of + slabs, slab_of)
    slab_of = jnp.where(slab_of > 2, slab_of - slabs, slab_of)
    walk_of = jnp.where(walk_of < -1, walk_of + walks, walk_of)
    walk_of = jnp.where(walk_of > 1, walk_of - walks, walk_of)
    row_parts = [
        profile(wrapped(first_row + r - at_row, grid_rows), radius) for r in range(rows)
    ]

    for copy in b_copies:
        copy.wait_recv()
    centre = jnp.zeros((groups, LANES), F32)
    for n, (i, j) in enumerate(offsets):
        table = picked[...] if (i, j) == (0, 0) else tables[n]
        value = jnp.take_along_axis(table, at_spot, axis=1)
        centre = jnp.where((slab_of == i) & (walk_of == j), value, centre)
    height = base * jnp.exp(-centre / TEMPER)
    row_parts = [height * part for part in row_parts]
    for r in range(rows):
        for group in range(groups):
            span = slice(group * LANES, (group + 1) * LANES)
            high, low = halves(near[:, span] * row_parts[r][group : group + 1])
            left_high[r * cols : (r + 1) * cols, span] = high
            left_low[r * cols : (r + 1) * cols, span] = low

    most = jnp.full((1, depth), -jnp.inf, F32)
    for r in range(rows):
        span = slice(r * cols, (r + 1) * cols)
        added = jnp.dot(left_high[span, :], right_high[...], preferred_element_type=F32)
        added += jnp.dot(left_low[span, :], right_high[...], preferred_element_type=F32)
        added += jnp.dot(left_high[span, :], right_low[...], preferred_element_type=F32)
        value = bias_ref[span, :] + added
        new_ref[span, :] = value
        most = jnp.maximum(most, jnp.max(value, axis=0, keepdims=True))
    top = most[:, 0:LANES]
    for i in range(1, depth // LANES):
        top = jnp.maximum(top, most[:, i * LANES : (i + 1) * LANES])
    top = jnp.where(over > 0, jnp.inf, top)
    peak[...] = top
    peaks[me] = top
    c_copies = [
        pltpu.make_async_remote_copy(
            peak, peaks.at[me], c_send.at[step], c_recv.at[step],
            device_id=place(step), device_id_type=MESH,
        )
        for step in range(1, devices)
    ]
    for copy in c_copies:
        copy.start()
    for copy in c_copies:
        copy.wait_recv()
    top_ref[...] = jnp.broadcast_to(jnp.max(peaks[...]), top_ref.shape)
    for copy in a_copies + b_copies + c_copies:
        copy.wait_send()


def by_kernel(per_group, collective_id, slabs, walks, arrays):
    bias_grid, hill_slab, hill_row, hill_col, hill_depth, hill_level, hill_count, table = arrays
    rows, cols, depth = bias_grid.shape
    devices = slabs * walks
    groups = devices // per_group
    total = groups * LANES
    cells = rows * cols
    vmem = pl.BlockSpec(memory_space=pltpu.VMEM)
    smem = pl.BlockSpec(memory_space=pltpu.SMEM)
    return pl.pallas_call(
        functools.partial(
            window_kernel, slabs, walks, rows, cols, table.shape[0], per_group
        ),
        out_shape=(
            jax.ShapeDtypeStruct((cells, depth), F32),
            jax.ShapeDtypeStruct((8, LANES), F32),
        ),
        in_specs=[vmem] * 6 + [smem] * 2,
        out_specs=(vmem, vmem),
        scratch_shapes=[
            pltpu.VMEM((8, LANES), F32),
            pltpu.VMEM((devices, 8, LANES), F32),
            pltpu.VMEM((cells, depth), BF16),
            pltpu.VMEM((cells, depth), BF16),
            pltpu.VMEM((groups, 8, LANES), F32),
            pltpu.VMEM((groups, LANES), F32),
            pltpu.VMEM((15, groups, LANES), F32),
            pltpu.VMEM((groups, 8, LANES), F32),
            pltpu.VMEM((cells, total), BF16),
            pltpu.VMEM((cells, total), BF16),
            pltpu.VMEM((total, depth), BF16),
            pltpu.VMEM((total, depth), BF16),
            pltpu.VMEM((cols, total), F32),
            pltpu.VMEM((1, LANES), F32),
            pltpu.VMEM((devices, 1, LANES), F32),
            pltpu.SemaphoreType.DMA((devices,)),
            pltpu.SemaphoreType.DMA((devices,)),
            pltpu.SemaphoreType.DMA((15,)),
            pltpu.SemaphoreType.DMA((15,)),
            pltpu.SemaphoreType.DMA((devices,)),
            pltpu.SemaphoreType.DMA((devices,)),
        ],
        compiler_params=pltpu.CompilerParams(
            collective_id=collective_id, has_side_effects=True
        ),
    )(
        bias_grid.reshape(cells, depth),
        hill_slab.reshape(hill_row.shape),
        hill_row,
        hill_col,
        hill_depth,
        hill_level,
        hill_count,
        table,
    )


def per_device(*arrays):
    bias_grid = arrays[0]
    shape = bias_grid.shape
    slabs, walks = lax.axis_size("slab"), lax.axis_size("walk")
    devices = slabs * walks
    fits = (
        arrays[2].size == LANES
        and slabs >= 5
        and walks >= 3
        and devices <= 64
        and devices % 4 == 0
        and shape[1] % LANES == 0
        and shape[1] >= 2 * shape[0]
        and shape[2] % LANES == 0
        and max(walks * shape[1], shape[2]) <= 4096
        and max(slabs * shape[0], arrays[7].size) <= 255
    )
    if not fits:
        return by_collectives(*arrays)

    def finish(new_bias, top):
        highest = top[0, 0]
        return new_bias.reshape(shape), FREE_SCALE * (highest - new_bias).reshape(shape)

    new_bias, top = by_kernel(4, 0, slabs, walks, arrays)
    return lax.cond(
        top[0, 0] == jnp.inf,
        lambda: finish(*by_kernel(1, 1, slabs, walks, arrays)),
        lambda: finish(new_bias, top),
    )


def solution(mesh):
    in_specs = (
        P("slab", "walk", None),
        P(("slab", "walk"), None, None),
        P(("slab", "walk"), None),
        P(("slab", "walk"), None),
        P(("slab", "walk"), None),
        P(("slab", "walk"), None),
        P(("slab", "walk")),
        P(),
    )
    out_specs = (P("slab", "walk", None), P("slab", "walk", None))
    return jax.shard_map(
        per_device, mesh=mesh, in_specs=in_specs, out_specs=out_specs, check_vma=False
    )
```

```python
import functools
import math

import jax
import jax.numpy as jnp
from jax import lax
from jax.experimental import pallas as pl
from jax.experimental.pallas import tpu as pltpu
from jax.sharding import PartitionSpec as P

BASE_HEIGHT = 1.2
TEMPER = 4.0
SIGMA_SHARE = 0.3125
FREE_SCALE = 10.0 / 9.0


def from_behind(block, axis, distance):
    devices = range(lax.axis_size(axis))
    route = [((i - distance) % len(devices), i) for i in devices]
    return lax.ppermute(block, axis, route)


def gaussian(position, centre, extent, radius):
    offset = jnp.mod(position - centre + extent // 2, extent) - extent // 2
    inside = (offset >= -radius) & (offset < radius)
    spread = SIGMA_SHARE * radius
    distance = offset.astype(jnp.float32)
    return jnp.where(inside, jnp.exp(-(distance * distance) / (2.0 * spread * spread)), 0.0)


def deposit(row_ids, col_ids, depth_ids, hill_lists, grid_rows, grid_cols, grid_depth, radius):
    slot_total = hill_lists.shape[1]
    block_size = math.gcd(slot_total, 256)
    row_count = row_ids.shape[0]
    col_count = col_ids.shape[0]
    depth_count = depth_ids.shape[0]

    def one_block(carry_sum, index):
        portion = lax.dynamic_slice_in_dim(hill_lists, index * block_size, block_size, 1)
        row_gauss = (
            gaussian(row_ids[:, None], portion[1].astype(jnp.int32)[None, :], grid_rows, radius)
            * portion[0][None, :]
        )
        col_gauss = gaussian(
            col_ids[:, None], portion[2].astype(jnp.int32)[None, :], grid_cols, radius
        )
        depth_gauss = gaussian(
            depth_ids[None, :], portion[3].astype(jnp.int32)[:, None], grid_depth, radius
        )
        plane_gauss = (row_gauss[:, None, :] * col_gauss[None, :, :]).reshape(
            row_count * col_count, block_size
        )
        added = jnp.dot(
            plane_gauss,
            depth_gauss,
            precision=lax.Precision.HIGHEST,
            preferred_element_type=jnp.float32,
        )
        return (carry_sum + added, None)

    start = jnp.zeros((row_count * col_count, depth_count), jnp.float32)
    result, unused = lax.scan(one_block, start, jnp.arange(slot_total // block_size))
    return result.reshape(row_count, col_count, depth_count)


def by_collectives(
    bias_grid, hill_slab, hill_row, hill_col, hill_depth, hill_level, hill_count, height_levels
):
    rows_dev, cols_dev, depth_bins = bias_grid.shape
    slab_count = lax.axis_size("slab")
    walk_count = lax.axis_size("walk")
    radius = 2 * rows_dev
    grid_rows = rows_dev * slab_count
    grid_cols = cols_dev * walk_count
    walkers_dev, hill_slots = hill_row.shape
    sent_rows = walkers_dev * hill_slots
    capacity = max(2, 4 * sent_rows // slab_count)
    target = hill_slab[:, :, 0].reshape(-1)
    centre_row = target * rows_dev + hill_row.reshape(-1)
    is_live = (
        lax.broadcasted_iota(jnp.int32, (walkers_dev, hill_slots), 1) < hill_count[:, None]
    ).reshape(-1)
    level_match = hill_level.reshape(-1)[:, None] == lax.broadcasted_iota(
        jnp.int32, (1, height_levels.shape[0]), 1
    )
    base_height = jnp.sum(jnp.where(level_match, height_levels[None, :], 0.0), axis=1)
    base_height = jnp.where(is_live, BASE_HEIGHT * base_height, 0.0)
    same_slab = target[:, None] == target[None, :]
    earlier = lax.broadcasted_iota(jnp.int32, (sent_rows, sent_rows), 1) < lax.broadcasted_iota(
        jnp.int32, (sent_rows, sent_rows), 0
    )
    slot_rank = jnp.sum((same_slab & earlier).astype(jnp.int32), axis=1)
    slot_place = target * capacity + slot_rank
    placing = (
        slot_place[:, None] == lax.broadcasted_iota(jnp.int32, (1, slab_count * capacity), 1)
    ).astype(jnp.float32)
    fields = jnp.stack(
        [
            base_height,
            centre_row.astype(jnp.float32),
            hill_col.reshape(-1).astype(jnp.float32),
            hill_depth.reshape(-1).astype(jnp.float32),
        ]
    )
    outgoing = jnp.dot(
        fields, placing, precision=lax.Precision.HIGHEST, preferred_element_type=jnp.float32
    )
    outgoing = outgoing.reshape(4, slab_count, capacity)
    arrived = lax.all_to_all(outgoing, "slab", split_axis=1, concat_axis=1, tiled=True).reshape(
        4, slab_count * capacity
    )
    shared = lax.all_gather(arrived, "walk", axis=1, tiled=True)
    slab_index = lax.axis_index("slab")
    walk_index = lax.axis_index("walk")
    local_row = jnp.clip(shared[1].astype(jnp.int32) - slab_index * rows_dev, 0, rows_dev - 1)
    local_col = shared[2].astype(jnp.int32) - walk_index * cols_dev
    local_depth = jnp.clip(shared[3].astype(jnp.int32), 0, depth_bins - 1)
    owned = (local_col >= 0) & (local_col < cols_dev)
    flat_place = (
        local_row * cols_dev + jnp.clip(local_col, 0, cols_dev - 1)
    ) * depth_bins + local_depth
    picked = bias_grid.reshape(-1)[flat_place]
    centre_value = lax.psum(jnp.where(owned, picked, 0.0), "walk")
    height = shared[0] * jnp.exp(-centre_value / TEMPER)
    hill_lists = jnp.stack([height, shared[1], shared[2], shared[3]])
    col_ids = walk_index * cols_dev + lax.broadcasted_iota(jnp.int32, (cols_dev,), 0)
    depth_ids = lax.broadcasted_iota(jnp.int32, (depth_bins,), 0)
    collected = [hill_lists]
    for offset in (-2, -1, 1, 2):
        collected.append(from_behind(hill_lists, "slab", offset))
    row_ids = slab_index * rows_dev + lax.broadcasted_iota(jnp.int32, (rows_dev,), 0)
    added = deposit(
        row_ids,
        col_ids,
        depth_ids,
        jnp.concatenate(collected, axis=1),
        grid_rows,
        grid_cols,
        depth_bins,
        radius,
    )
    new_bias = bias_grid + added
    highest = lax.pmax(jnp.max(new_bias), ("slab", "walk"))
    free_energy = FREE_SCALE * (highest - new_bias)
    return (new_bias, free_energy)


LANES = 128
F32 = jnp.float32
BF16 = jnp.bfloat16
MESH = pl.DeviceIdType.MESH
NT = (((1,), (1,)), ((), ()))


def wrapped(offset, extent):
    offset = jnp.where(offset >= extent // 2, offset - extent, offset)
    return jnp.where(offset < -(extent // 2), offset + extent, offset)


def profile(offset, radius):
    spread = SIGMA_SHARE * radius
    value = jnp.exp(-(offset * offset) / (2.0 * spread * spread))
    return jnp.where((offset >= -radius) & (offset < radius), value, 0.0)


def halves(value):
    high = value.astype(BF16)
    return high, (value - high.astype(F32)).astype(BF16)


def iota(shape, dim):
    return lax.broadcasted_iota(jnp.int32, shape, dim).astype(F32)


def window_kernel(
    slabs, walks, rows, cols, levels, per_group,
    bias_in, slab_in, row_in, col_in, depth_in, level_in, count_in, table_in,
    new_ref, top_ref, flag_ref,
    bias_ref, slab_ref, row_ref, col_ref, depth_ref, level_ref, count_ref, table_ref, in_sems,
    mine, hills, bias_high, bias_low, own, picked, tables, chosen,
    left_high, left_low, right_high, right_low, near, peak, peaks,
    a_send, a_recv, b_send, b_recv, c_send, c_recv,
):
    devices = slabs * walks
    groups = devices // per_group
    share = LANES // per_group
    cells, depth = bias_ref.shape
    radius = 2 * rows
    grid_rows, grid_cols = slabs * rows, walks * cols
    slab = lax.axis_index("slab")
    walk = lax.axis_index("walk")
    me = slab * walks + walk
    first_row = (slab * rows).astype(F32)
    first_col = (walk * cols).astype(F32)

    def place(step):
        other = lax.rem(me + step, devices)
        return (other // walks, lax.rem(other, walks))

    barrier = pltpu.get_barrier_semaphore()
    for step in range(1, devices):
        pl.semaphore_signal(barrier, inc=1, device_id=place(step), device_id_type=MESH)

    inputs = (
        (slab_in, slab_ref), (row_in, row_ref), (col_in, col_ref), (depth_in, depth_ref),
        (level_in, level_ref), (count_in, count_ref), (table_in, table_ref), (bias_in, bias_ref),
    )
    fetches = [
        pltpu.make_async_copy(there, here, in_sems.at[i])
        for i, (there, here) in enumerate(inputs)
    ]
    for fetch in fetches:
        fetch.start()
    for fetch in fetches[:-1]:
        fetch.wait()

    def in_row(ref):
        value = ref[...].astype(F32)
        return jnp.concatenate([value[i : i + 1] for i in range(value.shape[0])], axis=1)

    slots = row_ref.shape[1]
    lane = iota((1, LANES), 1)
    live = jnp.zeros((1, LANES), F32)
    for i in range(row_ref.shape[0]):
        inside = (lane >= i * slots) & (lane < i * slots + count_ref[i].astype(F32))
        live = jnp.where(inside, 1.0, live)
    target = in_row(slab_ref)
    centre_row = target * rows + in_row(row_ref)
    centre_col = in_row(col_ref)
    centre_depth = in_row(depth_ref)
    owner = target * walks + jnp.floor(centre_col / cols)
    owner = jnp.where(live > 0, owner, -1.0)
    owners = jnp.broadcast_to(owner, (LANES, LANES))
    same = (owners == owners.T) & (iota((LANES, LANES), 0) < iota((LANES, LANES), 1))
    rank = jnp.sum(jnp.where(same, 1.0, 0.0), axis=0, keepdims=True)
    over = jnp.max(jnp.where((live > 0) & (rank >= share), 1.0, 0.0))
    spot = rank + (lax.rem(me, per_group) * share).astype(F32)
    spot = jnp.where((live > 0) & (rank < share), spot, -1.0)
    col_high = jnp.floor(centre_col / 16.0)
    depth_high = jnp.floor(centre_depth / 16.0)
    fields = (
        jnp.where(live > 0, in_row(level_ref) + 1.0, 0.0),
        centre_row,
        col_high,
        centre_col - 16.0 * col_high,
        depth_high,
        centre_depth - 16.0 * depth_high,
        spot,
        live,
    )
    for i, field in enumerate(fields):
        mine[i : i + 1, :] = field
    hills[me] = mine[...]

    pl.semaphore_wait(barrier, devices - 1)
    a_copies = [
        pltpu.make_async_remote_copy(
            mine, hills.at[me], a_send.at[step], a_recv.at[step],
            device_id=place(step), device_id_type=MESH,
        )
        for step in range(1, devices)
    ]
    for copy in a_copies:
        copy.start()

    fetches[-1].wait()
    high, low = halves(bias_ref[...])
    bias_high[...] = high
    bias_low[...] = low
    earlier = jnp.where(
        iota((LANES, LANES), 0) < iota((LANES, LANES), 1), 1.0, 0.0
    ).astype(BF16)
    one, two = (
        lax.broadcasted_iota(jnp.int32, (devices, devices), 0),
        lax.broadcasted_iota(jnp.int32, (devices, devices), 1),
    )
    before = jnp.where((one // per_group == two // per_group) & (two < one), 1.0, 0.0).astype(BF16)

    for copy in a_copies:
        copy.wait_recv()

    there = hills[:, 7, :] > 0
    hill_row = hills[:, 1, :]
    hill_col = hills[:, 2, :] * 16.0 + hills[:, 3, :]
    away_row = hill_row - first_row
    away_col = hill_col - first_col
    owned = there & (away_row >= 0) & (away_row < rows) & (away_col >= 0) & (away_col < cols)
    own_place = jnp.where(owned, hills[:, 6, :], -1.0)

    def past(away, extent, limit):
        away = away + (radius - 1)
        away = jnp.where(away < 0, away + extent, away)
        away = jnp.where(away >= extent, away - extent, away)
        return away < limit

    close = (
        there
        & past(away_row, grid_rows, rows + 2 * radius - 1)
        & past(away_col, grid_cols, cols + 2 * radius - 1)
    )
    close_one = jnp.where(close, 1.0, 0.0)
    close_half = close_one.astype(BF16)
    rank_in = jnp.dot(close_half, earlier, preferred_element_type=F32)
    rank_of = jnp.sum(
        jnp.dot(before, close_half, preferred_element_type=F32), axis=1, keepdims=True
    )
    close_place = jnp.where(close, rank_in + rank_of, -1.0)
    over = jnp.maximum(over, jnp.max(jnp.where(close_place >= LANES, 1.0, 0.0)))

    slot = iota((LANES, per_group * LANES), 0)

    def group_fields(group):
        parts = [hills[group * per_group + i] for i in range(per_group)]
        return jnp.concatenate(parts, axis=1).astype(BF16)

    def group_places(places, group):
        parts = [
            places[group * per_group + i : group * per_group + i + 1, :] for i in range(per_group)
        ]
        matches = slot == jnp.concatenate(parts, axis=1)
        return jnp.where(matches, 1.0, 0.0).astype(BF16)

    for group in range(groups):
        own[group] = lax.dot_general(
            group_fields(group), group_places(own_place, group), NT, preferred_element_type=F32
        )

    cell_id = iota((cells, LANES), 0)
    depth_id = iota((depth, LANES), 0)

    def pick(group, carry):
        part = own[group]
        wanted = part[4:5] * 16.0 + part[5:6]
        select = jnp.where(depth_id == wanted, 1.0, 0.0).astype(BF16)
        lines = jnp.dot(bias_high[...], select, preferred_element_type=F32)
        lines = lines + jnp.dot(bias_low[...], select, preferred_element_type=F32)
        cell = (part[1:2] - first_row) * cols + part[2:3] * 16.0 + part[3:4] - first_col
        value = jnp.sum(jnp.where(cell_id == cell, lines, 0.0), axis=0, keepdims=True)
        picked[pl.ds(group, 1), :] = value
        return carry

    lax.fori_loop(0, groups, pick, 0, unroll=groups <= 8)

    offsets = [(i, j) for i in (-2, -1, 0, 1, 2) for j in (-1, 0, 1)]
    b_copies = []
    for n, (i, j) in enumerate(offsets):
        if (i, j) == (0, 0):
            continue
        device = (lax.rem(slab - i + slabs, slabs), lax.rem(walk - j + walks, walks))
        b_copies.append(
            pltpu.make_async_remote_copy(
                picked, tables.at[n], b_send.at[n], b_recv.at[n],
                device_id=device, device_id_type=MESH,
            )
        )
    for copy in b_copies:
        copy.start()

    depth_lane = iota((LANES, depth), 1)
    col_id = iota((cols, LANES), 0)
    for group in range(groups):
        data, places = group_fields(group), group_places(close_place, group)
        chosen[group] = lax.dot_general(data, places, NT, preferred_element_type=F32)
        column = lax.dot_general(places, data, NT, preferred_element_type=F32)
        at = column[:, 4:5] * 16.0 + column[:, 5:6]
        high, low = halves(profile(wrapped(depth_lane - at, depth), radius))
        right_high[group * LANES : (group + 1) * LANES, :] = high
        right_low[group * LANES : (group + 1) * LANES, :] = low
        part = chosen[group]
        at = part[2:3] * 16.0 + part[3:4]
        near[:, group * LANES : (group + 1) * LANES] = profile(
            wrapped(col_id + first_col - at, grid_cols), radius
        )

    level = chosen[:, 0, :]
    base = jnp.zeros((groups, LANES), F32)
    for i in range(levels):
        base = jnp.where(level == i + 1, BASE_HEIGHT * table_ref[i], base)
    at_row = chosen[:, 1, :]
    at_col = chosen[:, 2, :] * 16.0 + chosen[:, 3, :]
    at_spot = chosen[:, 6, :].astype(jnp.int32)
    slab_of = jnp.floor(at_row / rows) - slab.astype(F32)
    walk_of = jnp.floor(at_col / cols) - walk.astype(F32)
    slab_of = jnp.where(slab_of < -2, slab_of + slabs, slab_of)
    slab_of = jnp.where(slab_of > 2, slab_of - slabs, slab_of)
    walk_of = jnp.where(walk_of < -1, walk_of + walks, walk_of)
    walk_of = jnp.where(walk_of > 1, walk_of - walks, walk_of)
    row_parts = [
        profile(wrapped(first_row + r - at_row, grid_rows), radius) for r in range(rows)
    ]

    for copy in b_copies:
        copy.wait_recv()
    centre = jnp.zeros((groups, LANES), F32)
    for n, (i, j) in enumerate(offsets):
        table = picked[...] if (i, j) == (0, 0) else tables[n]
        value = jnp.take_along_axis(table, at_spot, axis=1)
        centre = jnp.where((slab_of == i) & (walk_of == j), value, centre)
    height = base * jnp.exp(-centre / TEMPER)
    row_parts = [height * part for part in row_parts]
    for r in range(rows):
        for group in range(groups):
            span = slice(group * LANES, (group + 1) * LANES)
            high, low = halves(near[:, span] * row_parts[r][group : group + 1])
            left_high[r * cols : (r + 1) * cols, span] = high
            left_low[r * cols : (r + 1) * cols, span] = low

    most = jnp.full((1, depth), -jnp.inf, F32)
    for r in range(rows):
        span = slice(r * cols, (r + 1) * cols)
        added = jnp.dot(left_high[span, :], right_high[...], preferred_element_type=F32)
        added += jnp.dot(left_low[span, :], right_high[...], preferred_element_type=F32)
        added += jnp.dot(left_high[span, :], right_low[...], preferred_element_type=F32)
        value = bias_ref[span, :] + added
        new_ref[span, :] = value
        most = jnp.maximum(most, jnp.max(value, axis=0, keepdims=True))
    top = most[:, 0:LANES]
    for i in range(1, depth // LANES):
        top = jnp.maximum(top, most[:, i * LANES : (i + 1) * LANES])
    top = jnp.where(over > 0, jnp.inf, top)
    peak[...] = top
    peaks[me] = top
    c_copies = [
        pltpu.make_async_remote_copy(
            peak, peaks.at[me], c_send.at[step], c_recv.at[step],
            device_id=place(step), device_id_type=MESH,
        )
        for step in range(1, devices)
    ]
    for copy in c_copies:
        copy.start()
    for copy in c_copies:
        copy.wait_recv()
    highest = jnp.max(peaks[...])
    top_ref[...] = jnp.broadcast_to(highest, top_ref.shape)
    flag_ref[0] = jnp.where(highest == jnp.inf, 1, 0)
    for copy in a_copies + b_copies + c_copies:
        copy.wait_send()


def by_kernel(per_group, collective_id, slabs, walks, arrays):
    bias_grid, hill_slab, hill_row, hill_col, hill_depth, hill_level, hill_count, table = arrays
    rows, cols, depth = bias_grid.shape
    devices = slabs * walks
    groups = devices // per_group
    total = groups * LANES
    cells = rows * cols
    walkers = hill_row.shape
    vmem = pl.BlockSpec(memory_space=pltpu.VMEM)
    smem = pl.BlockSpec(memory_space=pltpu.SMEM)
    hbm = pl.BlockSpec(memory_space=pltpu.HBM)
    return pl.pallas_call(
        functools.partial(
            window_kernel, slabs, walks, rows, cols, table.shape[0], per_group
        ),
        out_shape=(
            jax.ShapeDtypeStruct((cells, depth), F32),
            jax.ShapeDtypeStruct((8, LANES), F32),
            jax.ShapeDtypeStruct((1,), jnp.int32),
        ),
        in_specs=[hbm] * 8,
        out_specs=(vmem, vmem, smem),
        scratch_shapes=[
            pltpu.VMEM((cells, depth), F32),
            pltpu.VMEM(walkers, jnp.int32),
            pltpu.VMEM(walkers, jnp.int32),
            pltpu.VMEM(walkers, jnp.int32),
            pltpu.VMEM(walkers, jnp.int32),
            pltpu.VMEM(walkers, jnp.int32),
            pltpu.SMEM(hill_count.shape, jnp.int32),
            pltpu.SMEM(table.shape, F32),
            pltpu.SemaphoreType.DMA((8,)),
            pltpu.VMEM((8, LANES), F32),
            pltpu.VMEM((devices, 8, LANES), F32),
            pltpu.VMEM((cells, depth), BF16),
            pltpu.VMEM((cells, depth), BF16),
            pltpu.VMEM((groups, 8, LANES), F32),
            pltpu.VMEM((groups, LANES), F32),
            pltpu.VMEM((15, groups, LANES), F32),
            pltpu.VMEM((groups, 8, LANES), F32),
            pltpu.VMEM((cells, total), BF16),
            pltpu.VMEM((cells, total), BF16),
            pltpu.VMEM((total, depth), BF16),
            pltpu.VMEM((total, depth), BF16),
            pltpu.VMEM((cols, total), F32),
            pltpu.VMEM((1, LANES), F32),
            pltpu.VMEM((devices, 1, LANES), F32),
            pltpu.SemaphoreType.DMA((devices,)),
            pltpu.SemaphoreType.DMA((devices,)),
            pltpu.SemaphoreType.DMA((15,)),
            pltpu.SemaphoreType.DMA((15,)),
            pltpu.SemaphoreType.DMA((devices,)),
            pltpu.SemaphoreType.DMA((devices,)),
        ],
        compiler_params=pltpu.CompilerParams(
            collective_id=collective_id,
            has_side_effects=True,
            vmem_limit_bytes=(12 + 10 * 4 // per_group) * 2**20,
        ),
    )(
        bias_grid.reshape(cells, depth),
        hill_slab.reshape(hill_row.shape),
        hill_row,
        hill_col,
        hill_depth,
        hill_level,
        hill_count,
        table,
    )


def output_kernel(new_ref, top_ref, new_out, free_out, free_ref, sems):
    parts = 4
    span = new_ref.shape[0] // parts
    first = pltpu.make_async_copy(new_ref, new_out, sems.at[0])
    first.start()
    copies = [first]
    for i in range(parts):
        rows = pl.ds(i * span, span)
        free_ref[rows, :] = FREE_SCALE * (top_ref[0:1, 0:1] - new_ref[rows, :])
        copy = pltpu.make_async_copy(free_ref.at[rows], free_out.at[rows], sems.at[1 + i])
        copy.start()
        copies.append(copy)
    for copy in copies:
        copy.wait()


def outputs(new_bias, top):
    hbm = pl.BlockSpec(memory_space=pltpu.HBM)
    return pl.pallas_call(
        output_kernel,
        out_shape=(jax.ShapeDtypeStruct(new_bias.shape, F32),) * 2,
        in_specs=[pl.BlockSpec(memory_space=pltpu.VMEM)] * 2,
        out_specs=(hbm, hbm),
        scratch_shapes=[pltpu.VMEM(new_bias.shape, F32), pltpu.SemaphoreType.DMA((5,))],
        compiler_params=pltpu.CompilerParams(vmem_limit_bytes=4 * 2**20),
    )(new_bias, top)


def per_device(*arrays):
    bias_grid = arrays[0]
    shape = bias_grid.shape
    slabs, walks = lax.axis_size("slab"), lax.axis_size("walk")
    devices = slabs * walks
    fits = (
        arrays[2].size == LANES
        and slabs >= 5
        and walks >= 3
        and devices <= 64
        and devices % 4 == 0
        and shape[1] % LANES == 0
        and shape[1] >= 2 * shape[0]
        and shape[2] % LANES == 0
        and max(walks * shape[1], shape[2]) <= 4096
        and max(slabs * shape[0], arrays[7].size) <= 255
    )
    if not fits:
        return by_collectives(*arrays)

    def finish(new_bias, top):
        new_out, free_out = outputs(new_bias, top)
        return new_out.reshape(shape), free_out.reshape(shape)

    new_bias, top, flag = by_kernel(4, 0, slabs, walks, arrays)
    return lax.cond(
        flag.reshape(()),
        lambda: finish(*by_kernel(1, 1, slabs, walks, arrays)[:2]),
        lambda: finish(new_bias, top),
    )


def solution(mesh):
    in_specs = (
        P("slab", "walk", None),
        P(("slab", "walk"), None, None),
        P(("slab", "walk"), None),
        P(("slab", "walk"), None),
        P(("slab", "walk"), None),
        P(("slab", "walk"), None),
        P(("slab", "walk")),
        P(),
    )
    out_specs = (P("slab", "walk", None), P("slab", "walk", None))
    return jax.shard_map(
        per_device, mesh=mesh, in_specs=in_specs, out_specs=out_specs, check_vma=False
    )
```

```python
import functools
import math

import jax
import jax.numpy as jnp
from jax import lax
from jax.experimental import pallas as pl
from jax.experimental.pallas import tpu as pltpu
from jax.sharding import PartitionSpec as P

BASE_HEIGHT = 1.2
TEMPER = 4.0
SIGMA_SHARE = 0.3125
FREE_SCALE = 10.0 / 9.0


def from_behind(block, axis, distance):
    devices = range(lax.axis_size(axis))
    route = [((i - distance) % len(devices), i) for i in devices]
    return lax.ppermute(block, axis, route)


def gaussian(position, centre, extent, radius):
    offset = jnp.mod(position - centre + extent // 2, extent) - extent // 2
    inside = (offset >= -radius) & (offset < radius)
    spread = SIGMA_SHARE * radius
    distance = offset.astype(jnp.float32)
    return jnp.where(inside, jnp.exp(-(distance * distance) / (2.0 * spread * spread)), 0.0)


def deposit(row_ids, col_ids, depth_ids, hill_lists, grid_rows, grid_cols, grid_depth, radius):
    slot_total = hill_lists.shape[1]
    block_size = math.gcd(slot_total, 256)
    row_count = row_ids.shape[0]
    col_count = col_ids.shape[0]
    depth_count = depth_ids.shape[0]

    def one_block(carry_sum, index):
        portion = lax.dynamic_slice_in_dim(hill_lists, index * block_size, block_size, 1)
        row_gauss = (
            gaussian(row_ids[:, None], portion[1].astype(jnp.int32)[None, :], grid_rows, radius)
            * portion[0][None, :]
        )
        col_gauss = gaussian(
            col_ids[:, None], portion[2].astype(jnp.int32)[None, :], grid_cols, radius
        )
        depth_gauss = gaussian(
            depth_ids[None, :], portion[3].astype(jnp.int32)[:, None], grid_depth, radius
        )
        plane_gauss = (row_gauss[:, None, :] * col_gauss[None, :, :]).reshape(
            row_count * col_count, block_size
        )
        added = jnp.dot(
            plane_gauss,
            depth_gauss,
            precision=lax.Precision.HIGHEST,
            preferred_element_type=jnp.float32,
        )
        return (carry_sum + added, None)

    start = jnp.zeros((row_count * col_count, depth_count), jnp.float32)
    result, unused = lax.scan(one_block, start, jnp.arange(slot_total // block_size))
    return result.reshape(row_count, col_count, depth_count)


def by_collectives(
    bias_grid, hill_slab, hill_row, hill_col, hill_depth, hill_level, hill_count, height_levels
):
    rows_dev, cols_dev, depth_bins = bias_grid.shape
    slab_count = lax.axis_size("slab")
    walk_count = lax.axis_size("walk")
    radius = 2 * rows_dev
    grid_rows = rows_dev * slab_count
    grid_cols = cols_dev * walk_count
    walkers_dev, hill_slots = hill_row.shape
    sent_rows = walkers_dev * hill_slots
    capacity = max(2, 4 * sent_rows // slab_count)
    target = hill_slab[:, :, 0].reshape(-1)
    centre_row = target * rows_dev + hill_row.reshape(-1)
    is_live = (
        lax.broadcasted_iota(jnp.int32, (walkers_dev, hill_slots), 1) < hill_count[:, None]
    ).reshape(-1)
    level_match = hill_level.reshape(-1)[:, None] == lax.broadcasted_iota(
        jnp.int32, (1, height_levels.shape[0]), 1
    )
    base_height = jnp.sum(jnp.where(level_match, height_levels[None, :], 0.0), axis=1)
    base_height = jnp.where(is_live, BASE_HEIGHT * base_height, 0.0)
    same_slab = target[:, None] == target[None, :]
    earlier = lax.broadcasted_iota(jnp.int32, (sent_rows, sent_rows), 1) < lax.broadcasted_iota(
        jnp.int32, (sent_rows, sent_rows), 0
    )
    slot_rank = jnp.sum((same_slab & earlier).astype(jnp.int32), axis=1)
    slot_place = target * capacity + slot_rank
    placing = (
        slot_place[:, None] == lax.broadcasted_iota(jnp.int32, (1, slab_count * capacity), 1)
    ).astype(jnp.float32)
    fields = jnp.stack(
        [
            base_height,
            centre_row.astype(jnp.float32),
            hill_col.reshape(-1).astype(jnp.float32),
            hill_depth.reshape(-1).astype(jnp.float32),
        ]
    )
    outgoing = jnp.dot(
        fields, placing, precision=lax.Precision.HIGHEST, preferred_element_type=jnp.float32
    )
    outgoing = outgoing.reshape(4, slab_count, capacity)
    arrived = lax.all_to_all(outgoing, "slab", split_axis=1, concat_axis=1, tiled=True).reshape(
        4, slab_count * capacity
    )
    shared = lax.all_gather(arrived, "walk", axis=1, tiled=True)
    slab_index = lax.axis_index("slab")
    walk_index = lax.axis_index("walk")
    local_row = jnp.clip(shared[1].astype(jnp.int32) - slab_index * rows_dev, 0, rows_dev - 1)
    local_col = shared[2].astype(jnp.int32) - walk_index * cols_dev
    local_depth = jnp.clip(shared[3].astype(jnp.int32), 0, depth_bins - 1)
    owned = (local_col >= 0) & (local_col < cols_dev)
    flat_place = (
        local_row * cols_dev + jnp.clip(local_col, 0, cols_dev - 1)
    ) * depth_bins + local_depth
    picked = bias_grid.reshape(-1)[flat_place]
    centre_value = lax.psum(jnp.where(owned, picked, 0.0), "walk")
    height = shared[0] * jnp.exp(-centre_value / TEMPER)
    hill_lists = jnp.stack([height, shared[1], shared[2], shared[3]])
    col_ids = walk_index * cols_dev + lax.broadcasted_iota(jnp.int32, (cols_dev,), 0)
    depth_ids = lax.broadcasted_iota(jnp.int32, (depth_bins,), 0)
    collected = [hill_lists]
    for offset in (-2, -1, 1, 2):
        collected.append(from_behind(hill_lists, "slab", offset))
    row_ids = slab_index * rows_dev + lax.broadcasted_iota(jnp.int32, (rows_dev,), 0)
    added = deposit(
        row_ids,
        col_ids,
        depth_ids,
        jnp.concatenate(collected, axis=1),
        grid_rows,
        grid_cols,
        depth_bins,
        radius,
    )
    new_bias = bias_grid + added
    highest = lax.pmax(jnp.max(new_bias), ("slab", "walk"))
    free_energy = FREE_SCALE * (highest - new_bias)
    return (new_bias, free_energy)


LANES = 128
F32 = jnp.float32
BF16 = jnp.bfloat16
MESH = pl.DeviceIdType.MESH
NT = (((1,), (1,)), ((), ()))


def wrapped(offset, extent):
    offset = jnp.where(offset >= extent // 2, offset - extent, offset)
    return jnp.where(offset < -(extent // 2), offset + extent, offset)


def profile(offset, radius):
    spread = SIGMA_SHARE * radius
    value = jnp.exp(-(offset * offset) / (2.0 * spread * spread))
    return jnp.where((offset >= -radius) & (offset < radius), value, 0.0)


def halves(value):
    high = value.astype(BF16)
    return high, (value - high.astype(F32)).astype(BF16)


def iota(shape, dim):
    return lax.broadcasted_iota(jnp.int32, shape, dim).astype(F32)


def window_kernel(
    slabs, walks, rows, cols, levels, per_group,
    bias_in, slab_in, row_in, col_in, depth_in, level_in, count_in, table_in,
    new_ref, top_ref, flag_ref,
    bias_ref, slab_ref, row_ref, col_ref, depth_ref, level_ref, count_ref, table_ref, in_sems,
    mine, hills, bias_high, bias_low, own, picked, tables, chosen,
    left_high, left_low, right_high, right_low, near, peak, peaks,
    a_send, a_recv, b_send, b_recv, c_send, c_recv,
):
    devices = slabs * walks
    groups = devices // per_group
    share = LANES // per_group
    cells, depth = bias_ref.shape
    radius = 2 * rows
    grid_rows, grid_cols = slabs * rows, walks * cols
    slab = lax.axis_index("slab")
    walk = lax.axis_index("walk")
    me = slab * walks + walk
    first_row = (slab * rows).astype(F32)
    first_col = (walk * cols).astype(F32)

    def place(step):
        other = lax.rem(me + step, devices)
        return (other // walks, lax.rem(other, walks))

    barrier = pltpu.get_barrier_semaphore()
    for step in range(1, devices):
        pl.semaphore_signal(barrier, inc=1, device_id=place(step), device_id_type=MESH)

    inputs = (
        (slab_in, slab_ref), (row_in, row_ref), (col_in, col_ref), (depth_in, depth_ref),
        (level_in, level_ref), (count_in, count_ref), (table_in, table_ref), (bias_in, bias_ref),
    )
    fetches = [
        pltpu.make_async_copy(there, here, in_sems.at[i])
        for i, (there, here) in enumerate(inputs)
    ]
    for fetch in fetches:
        fetch.start()
    for fetch in fetches[:-1]:
        fetch.wait()

    def in_row(ref):
        value = ref[...].astype(F32)
        return jnp.concatenate([value[i : i + 1] for i in range(value.shape[0])], axis=1)

    slots = row_ref.shape[1]
    lane = iota((1, LANES), 1)
    live = jnp.zeros((1, LANES), F32)
    for i in range(row_ref.shape[0]):
        inside = (lane >= i * slots) & (lane < i * slots + count_ref[i].astype(F32))
        live = jnp.where(inside, 1.0, live)
    target = in_row(slab_ref)
    centre_row = target * rows + in_row(row_ref)
    centre_col = in_row(col_ref)
    centre_depth = in_row(depth_ref)
    owner = target * walks + jnp.floor(centre_col / cols)
    owner = jnp.where(live > 0, owner, -1.0)
    owners = jnp.broadcast_to(owner, (LANES, LANES))
    same = (owners == owners.T) & (iota((LANES, LANES), 0) < iota((LANES, LANES), 1))
    rank = jnp.sum(jnp.where(same, 1.0, 0.0), axis=0, keepdims=True)
    over = jnp.max(jnp.where((live > 0) & (rank >= share), 1.0, 0.0))
    spot = rank + (lax.rem(me, per_group) * share).astype(F32)
    spot = jnp.where((live > 0) & (rank < share), spot, -1.0)
    col_high = jnp.floor(centre_col / 16.0)
    depth_high = jnp.floor(centre_depth / 16.0)
    fields = (
        jnp.where(live > 0, in_row(level_ref) + 1.0, 0.0),
        centre_row,
        col_high,
        centre_col - 16.0 * col_high,
        depth_high,
        centre_depth - 16.0 * depth_high,
        spot,
        live,
    )
    for i, field in enumerate(fields):
        mine[i : i + 1, :] = field
    hills[me] = mine[...]

    pl.semaphore_wait(barrier, devices - 1)
    a_copies = [
        pltpu.make_async_remote_copy(
            mine, hills.at[me], a_send.at[step], a_recv.at[step],
            device_id=place(step), device_id_type=MESH,
        )
        for step in range(1, devices)
    ]
    for copy in a_copies:
        copy.start()

    fetches[-1].wait()
    high, low = halves(bias_ref[...])
    bias_high[...] = high
    bias_low[...] = low
    earlier = jnp.where(
        iota((LANES, LANES), 0) < iota((LANES, LANES), 1), 1.0, 0.0
    ).astype(BF16)
    one, two = (
        lax.broadcasted_iota(jnp.int32, (devices, devices), 0),
        lax.broadcasted_iota(jnp.int32, (devices, devices), 1),
    )
    before = jnp.where((one // per_group == two // per_group) & (two < one), 1.0, 0.0).astype(BF16)

    for copy in a_copies:
        copy.wait_recv()

    there = hills[:, 7, :] > 0
    hill_row = hills[:, 1, :]
    hill_col = hills[:, 2, :] * 16.0 + hills[:, 3, :]
    away_row = hill_row - first_row
    away_col = hill_col - first_col
    owned = there & (away_row >= 0) & (away_row < rows) & (away_col >= 0) & (away_col < cols)
    own_place = jnp.where(owned, hills[:, 6, :], -1.0)

    def past(away, extent, limit):
        away = away + (radius - 1)
        away = jnp.where(away < 0, away + extent, away)
        away = jnp.where(away >= extent, away - extent, away)
        return away < limit

    close = (
        there
        & past(away_row, grid_rows, rows + 2 * radius - 1)
        & past(away_col, grid_cols, cols + 2 * radius - 1)
    )
    close_one = jnp.where(close, 1.0, 0.0)
    close_half = close_one.astype(BF16)
    rank_in = jnp.dot(close_half, earlier, preferred_element_type=F32)
    rank_of = jnp.sum(
        jnp.dot(before, close_half, preferred_element_type=F32), axis=1, keepdims=True
    )
    close_place = jnp.where(close, rank_in + rank_of, -1.0)
    over = jnp.maximum(over, jnp.max(jnp.where(close_place >= LANES, 1.0, 0.0)))

    slot = iota((LANES, per_group * LANES), 0)

    def group_fields(group):
        parts = [hills[group * per_group + i] for i in range(per_group)]
        return jnp.concatenate(parts, axis=1).astype(BF16)

    def group_places(places, group):
        parts = [
            places[group * per_group + i : group * per_group + i + 1, :] for i in range(per_group)
        ]
        matches = slot == jnp.concatenate(parts, axis=1)
        return jnp.where(matches, 1.0, 0.0).astype(BF16)

    for group in range(groups):
        own[group] = lax.dot_general(
            group_fields(group), group_places(own_place, group), NT, preferred_element_type=F32
        )

    cell_id = iota((cells, 2 * LANES), 0)
    depth_id = iota((depth, 2 * LANES), 0)

    def pick(pair, carry):
        part = jnp.concatenate([own[2 * pair], own[2 * pair + 1]], axis=1)
        wanted = part[4:5] * 16.0 + part[5:6]
        select = jnp.where(depth_id == wanted, 1.0, 0.0).astype(BF16)
        lines = jnp.dot(bias_high[...], select, preferred_element_type=F32)
        lines = lines + jnp.dot(bias_low[...], select, preferred_element_type=F32)
        cell = (part[1:2] - first_row) * cols + part[2:3] * 16.0 + part[3:4] - first_col
        value = jnp.sum(jnp.where(cell_id == cell, lines, 0.0), axis=0, keepdims=True)
        picked[pl.ds(2 * pair, 1), :] = value[:, :LANES]
        picked[pl.ds(2 * pair + 1, 1), :] = value[:, LANES:]
        return carry

    lax.fori_loop(0, groups // 2, pick, 0, unroll=groups <= 8)

    offsets = [(i, j) for i in (-2, -1, 0, 1, 2) for j in (-1, 0, 1)]
    b_copies = []
    for n, (i, j) in enumerate(offsets):
        if (i, j) == (0, 0):
            continue
        device = (lax.rem(slab - i + slabs, slabs), lax.rem(walk - j + walks, walks))
        b_copies.append(
            pltpu.make_async_remote_copy(
                picked, tables.at[n], b_send.at[n], b_recv.at[n],
                device_id=device, device_id_type=MESH,
            )
        )
    for copy in b_copies:
        copy.start()

    depth_lane = iota((LANES, depth), 1)
    col_id = iota((cols, LANES), 0)
    for group in range(groups):
        data, places = group_fields(group), group_places(close_place, group)
        chosen[group] = lax.dot_general(data, places, NT, preferred_element_type=F32)
        column = lax.dot_general(places, data, NT, preferred_element_type=F32)
        at = column[:, 4:5] * 16.0 + column[:, 5:6]
        high, low = halves(profile(wrapped(depth_lane - at, depth), radius))
        right_high[group * LANES : (group + 1) * LANES, :] = high
        right_low[group * LANES : (group + 1) * LANES, :] = low
        part = chosen[group]
        at = part[2:3] * 16.0 + part[3:4]
        near[:, group * LANES : (group + 1) * LANES] = profile(
            wrapped(col_id + first_col - at, grid_cols), radius
        )

    level = chosen[:, 0, :]
    base = jnp.zeros((groups, LANES), F32)
    for i in range(levels):
        base = jnp.where(level == i + 1, BASE_HEIGHT * table_ref[i], base)
    at_row = chosen[:, 1, :]
    at_col = chosen[:, 2, :] * 16.0 + chosen[:, 3, :]
    at_spot = chosen[:, 6, :].astype(jnp.int32)
    slab_of = jnp.floor(at_row / rows) - slab.astype(F32)
    walk_of = jnp.floor(at_col / cols) - walk.astype(F32)
    slab_of = jnp.where(slab_of < -2, slab_of + slabs, slab_of)
    slab_of = jnp.where(slab_of > 2, slab_of - slabs, slab_of)
    walk_of = jnp.where(walk_of < -1, walk_of + walks, walk_of)
    walk_of = jnp.where(walk_of > 1, walk_of - walks, walk_of)
    row_parts = [
        profile(wrapped(first_row + r - at_row, grid_rows), radius) for r in range(rows)
    ]

    for copy in b_copies:
        copy.wait_recv()
    centre = jnp.zeros((groups, LANES), F32)
    for n, (i, j) in enumerate(offsets):
        table = picked[...] if (i, j) == (0, 0) else tables[n]
        value = jnp.take_along_axis(table, at_spot, axis=1)
        centre = jnp.where((slab_of == i) & (walk_of == j), value, centre)
    height = base * jnp.exp(-centre / TEMPER)
    row_parts = [height * part for part in row_parts]
    for r in range(rows):
        for group in range(groups):
            span = slice(group * LANES, (group + 1) * LANES)
            high, low = halves(near[:, span] * row_parts[r][group : group + 1])
            left_high[r * cols : (r + 1) * cols, span] = high
            left_low[r * cols : (r + 1) * cols, span] = low

    added = jnp.dot(left_high[...], right_high[...], preferred_element_type=F32)
    added += jnp.dot(left_low[...], right_high[...], preferred_element_type=F32)
    added += jnp.dot(left_high[...], right_low[...], preferred_element_type=F32)
    value = bias_ref[...] + added
    new_ref[...] = value
    most = jnp.max(value, axis=0, keepdims=True)
    top = most[:, 0:LANES]
    for i in range(1, depth // LANES):
        top = jnp.maximum(top, most[:, i * LANES : (i + 1) * LANES])
    top = jnp.where(over > 0, jnp.inf, top)
    peak[...] = top
    peaks[me] = top
    c_copies = [
        pltpu.make_async_remote_copy(
            peak, peaks.at[me], c_send.at[step], c_recv.at[step],
            device_id=place(step), device_id_type=MESH,
        )
        for step in range(1, devices)
    ]
    for copy in c_copies:
        copy.start()
    for copy in c_copies:
        copy.wait_recv()
    highest = jnp.max(peaks[...])
    top_ref[...] = jnp.broadcast_to(highest, top_ref.shape)
    flag_ref[0] = jnp.where(highest == jnp.inf, 1, 0)
    for copy in a_copies + b_copies + c_copies:
        copy.wait_send()


def by_kernel(per_group, collective_id, slabs, walks, arrays):
    bias_grid, hill_slab, hill_row, hill_col, hill_depth, hill_level, hill_count, table = arrays
    rows, cols, depth = bias_grid.shape
    devices = slabs * walks
    groups = devices // per_group
    total = groups * LANES
    cells = rows * cols
    walkers = hill_row.shape
    vmem = pl.BlockSpec(memory_space=pltpu.VMEM)
    smem = pl.BlockSpec(memory_space=pltpu.SMEM)
    hbm = pl.BlockSpec(memory_space=pltpu.HBM)
    return pl.pallas_call(
        functools.partial(
            window_kernel, slabs, walks, rows, cols, table.shape[0], per_group
        ),
        out_shape=(
            jax.ShapeDtypeStruct((cells, depth), F32),
            jax.ShapeDtypeStruct((8, LANES), F32),
            jax.ShapeDtypeStruct((1,), jnp.int32),
        ),
        in_specs=[hbm] * 8,
        out_specs=(vmem, vmem, smem),
        scratch_shapes=[
            pltpu.VMEM((cells, depth), F32),
            pltpu.VMEM(walkers, jnp.int32),
            pltpu.VMEM(walkers, jnp.int32),
            pltpu.VMEM(walkers, jnp.int32),
            pltpu.VMEM(walkers, jnp.int32),
            pltpu.VMEM(walkers, jnp.int32),
            pltpu.SMEM(hill_count.shape, jnp.int32),
            pltpu.SMEM(table.shape, F32),
            pltpu.SemaphoreType.DMA((8,)),
            pltpu.VMEM((8, LANES), F32),
            pltpu.VMEM((devices, 8, LANES), F32),
            pltpu.VMEM((cells, depth), BF16),
            pltpu.VMEM((cells, depth), BF16),
            pltpu.VMEM((groups, 8, LANES), F32),
            pltpu.VMEM((groups, LANES), F32),
            pltpu.VMEM((15, groups, LANES), F32),
            pltpu.VMEM((groups, 8, LANES), F32),
            pltpu.VMEM((cells, total), BF16),
            pltpu.VMEM((cells, total), BF16),
            pltpu.VMEM((total, depth), BF16),
            pltpu.VMEM((total, depth), BF16),
            pltpu.VMEM((cols, total), F32),
            pltpu.VMEM((1, LANES), F32),
            pltpu.VMEM((devices, 1, LANES), F32),
            pltpu.SemaphoreType.DMA((devices,)),
            pltpu.SemaphoreType.DMA((devices,)),
            pltpu.SemaphoreType.DMA((15,)),
            pltpu.SemaphoreType.DMA((15,)),
            pltpu.SemaphoreType.DMA((devices,)),
            pltpu.SemaphoreType.DMA((devices,)),
        ],
        compiler_params=pltpu.CompilerParams(
            collective_id=collective_id,
            has_side_effects=True,
            vmem_limit_bytes=(12 + 10 * 4 // per_group) * 2**20,
        ),
    )(
        bias_grid.reshape(cells, depth),
        hill_slab.reshape(hill_row.shape),
        hill_row,
        hill_col,
        hill_depth,
        hill_level,
        hill_count,
        table,
    )


def output_kernel(new_ref, top_ref, new_out, free_out, free_ref, sems):
    parts = 4
    span = new_ref.shape[0] // parts
    first = pltpu.make_async_copy(new_ref, new_out, sems.at[0])
    first.start()
    copies = [first]
    for i in range(parts):
        rows = pl.ds(i * span, span)
        free_ref[rows, :] = FREE_SCALE * (top_ref[0:1, 0:1] - new_ref[rows, :])
        copy = pltpu.make_async_copy(free_ref.at[rows], free_out.at[rows], sems.at[1 + i])
        copy.start()
        copies.append(copy)
    for copy in copies:
        copy.wait()


def outputs(new_bias, top):
    hbm = pl.BlockSpec(memory_space=pltpu.HBM)
    return pl.pallas_call(
        output_kernel,
        out_shape=(jax.ShapeDtypeStruct(new_bias.shape, F32),) * 2,
        in_specs=[pl.BlockSpec(memory_space=pltpu.VMEM)] * 2,
        out_specs=(hbm, hbm),
        scratch_shapes=[pltpu.VMEM(new_bias.shape, F32), pltpu.SemaphoreType.DMA((5,))],
        compiler_params=pltpu.CompilerParams(vmem_limit_bytes=4 * 2**20),
    )(new_bias, top)


def per_device(*arrays):
    bias_grid = arrays[0]
    shape = bias_grid.shape
    slabs, walks = lax.axis_size("slab"), lax.axis_size("walk")
    devices = slabs * walks
    fits = (
        arrays[2].size == LANES
        and slabs >= 5
        and walks >= 3
        and devices <= 64
        and devices % 8 == 0
        and shape[1] % LANES == 0
        and shape[1] >= 2 * shape[0]
        and shape[2] % LANES == 0
        and max(walks * shape[1], shape[2]) <= 4096
        and max(slabs * shape[0], arrays[7].size) <= 255
    )
    if not fits:
        return by_collectives(*arrays)

    def finish(new_bias, top):
        new_out, free_out = outputs(new_bias, top)
        return new_out.reshape(shape), free_out.reshape(shape)

    new_bias, top, flag = by_kernel(4, 0, slabs, walks, arrays)
    return lax.cond(
        flag.reshape(()),
        lambda: finish(*by_kernel(1, 1, slabs, walks, arrays)[:2]),
        lambda: finish(new_bias, top),
    )


def solution(mesh):
    in_specs = (
        P("slab", "walk", None),
        P(("slab", "walk"), None, None),
        P(("slab", "walk"), None),
        P(("slab", "walk"), None),
        P(("slab", "walk"), None),
        P(("slab", "walk"), None),
        P(("slab", "walk")),
        P(),
    )
    out_specs = (P("slab", "walk", None), P("slab", "walk", None))
    return jax.shard_map(
        per_device, mesh=mesh, in_specs=in_specs, out_specs=out_specs, check_vma=False
    )
```

```python
import functools
import math

import jax
import jax.numpy as jnp
from jax import lax
from jax.experimental import pallas as pl
from jax.experimental.pallas import tpu as pltpu
from jax.sharding import PartitionSpec as P

BASE_HEIGHT = 1.2
TEMPER = 4.0
SIGMA_SHARE = 0.3125
FREE_SCALE = 10.0 / 9.0


def from_behind(block, axis, distance):
    devices = range(lax.axis_size(axis))
    route = [((i - distance) % len(devices), i) for i in devices]
    return lax.ppermute(block, axis, route)


def gaussian(position, centre, extent, radius):
    offset = jnp.mod(position - centre + extent // 2, extent) - extent // 2
    inside = (offset >= -radius) & (offset < radius)
    spread = SIGMA_SHARE * radius
    distance = offset.astype(jnp.float32)
    return jnp.where(inside, jnp.exp(-(distance * distance) / (2.0 * spread * spread)), 0.0)


def deposit(row_ids, col_ids, depth_ids, hill_lists, grid_rows, grid_cols, grid_depth, radius):
    slot_total = hill_lists.shape[1]
    block_size = math.gcd(slot_total, 256)
    row_count = row_ids.shape[0]
    col_count = col_ids.shape[0]
    depth_count = depth_ids.shape[0]

    def one_block(carry_sum, index):
        portion = lax.dynamic_slice_in_dim(hill_lists, index * block_size, block_size, 1)
        row_gauss = (
            gaussian(row_ids[:, None], portion[1].astype(jnp.int32)[None, :], grid_rows, radius)
            * portion[0][None, :]
        )
        col_gauss = gaussian(
            col_ids[:, None], portion[2].astype(jnp.int32)[None, :], grid_cols, radius
        )
        depth_gauss = gaussian(
            depth_ids[None, :], portion[3].astype(jnp.int32)[:, None], grid_depth, radius
        )
        plane_gauss = (row_gauss[:, None, :] * col_gauss[None, :, :]).reshape(
            row_count * col_count, block_size
        )
        added = jnp.dot(
            plane_gauss,
            depth_gauss,
            precision=lax.Precision.HIGHEST,
            preferred_element_type=jnp.float32,
        )
        return (carry_sum + added, None)

    start = jnp.zeros((row_count * col_count, depth_count), jnp.float32)
    result, unused = lax.scan(one_block, start, jnp.arange(slot_total // block_size))
    return result.reshape(row_count, col_count, depth_count)


def by_collectives(
    bias_grid, hill_slab, hill_row, hill_col, hill_depth, hill_level, hill_count, height_levels
):
    rows_dev, cols_dev, depth_bins = bias_grid.shape
    slab_count = lax.axis_size("slab")
    walk_count = lax.axis_size("walk")
    radius = 2 * rows_dev
    grid_rows = rows_dev * slab_count
    grid_cols = cols_dev * walk_count
    walkers_dev, hill_slots = hill_row.shape
    sent_rows = walkers_dev * hill_slots
    capacity = max(2, 4 * sent_rows // slab_count)
    target = hill_slab[:, :, 0].reshape(-1)
    centre_row = target * rows_dev + hill_row.reshape(-1)
    is_live = (
        lax.broadcasted_iota(jnp.int32, (walkers_dev, hill_slots), 1) < hill_count[:, None]
    ).reshape(-1)
    level_match = hill_level.reshape(-1)[:, None] == lax.broadcasted_iota(
        jnp.int32, (1, height_levels.shape[0]), 1
    )
    base_height = jnp.sum(jnp.where(level_match, height_levels[None, :], 0.0), axis=1)
    base_height = jnp.where(is_live, BASE_HEIGHT * base_height, 0.0)
    same_slab = target[:, None] == target[None, :]
    earlier = lax.broadcasted_iota(jnp.int32, (sent_rows, sent_rows), 1) < lax.broadcasted_iota(
        jnp.int32, (sent_rows, sent_rows), 0
    )
    slot_rank = jnp.sum((same_slab & earlier).astype(jnp.int32), axis=1)
    slot_place = target * capacity + slot_rank
    placing = (
        slot_place[:, None] == lax.broadcasted_iota(jnp.int32, (1, slab_count * capacity), 1)
    ).astype(jnp.float32)
    fields = jnp.stack(
        [
            base_height,
            centre_row.astype(jnp.float32),
            hill_col.reshape(-1).astype(jnp.float32),
            hill_depth.reshape(-1).astype(jnp.float32),
        ]
    )
    outgoing = jnp.dot(
        fields, placing, precision=lax.Precision.HIGHEST, preferred_element_type=jnp.float32
    )
    outgoing = outgoing.reshape(4, slab_count, capacity)
    arrived = lax.all_to_all(outgoing, "slab", split_axis=1, concat_axis=1, tiled=True).reshape(
        4, slab_count * capacity
    )
    shared = lax.all_gather(arrived, "walk", axis=1, tiled=True)
    slab_index = lax.axis_index("slab")
    walk_index = lax.axis_index("walk")
    local_row = jnp.clip(shared[1].astype(jnp.int32) - slab_index * rows_dev, 0, rows_dev - 1)
    local_col = shared[2].astype(jnp.int32) - walk_index * cols_dev
    local_depth = jnp.clip(shared[3].astype(jnp.int32), 0, depth_bins - 1)
    owned = (local_col >= 0) & (local_col < cols_dev)
    flat_place = (
        local_row * cols_dev + jnp.clip(local_col, 0, cols_dev - 1)
    ) * depth_bins + local_depth
    picked = bias_grid.reshape(-1)[flat_place]
    centre_value = lax.psum(jnp.where(owned, picked, 0.0), "walk")
    height = shared[0] * jnp.exp(-centre_value / TEMPER)
    hill_lists = jnp.stack([height, shared[1], shared[2], shared[3]])
    col_ids = walk_index * cols_dev + lax.broadcasted_iota(jnp.int32, (cols_dev,), 0)
    depth_ids = lax.broadcasted_iota(jnp.int32, (depth_bins,), 0)
    collected = [hill_lists]
    for offset in (-2, -1, 1, 2):
        collected.append(from_behind(hill_lists, "slab", offset))
    row_ids = slab_index * rows_dev + lax.broadcasted_iota(jnp.int32, (rows_dev,), 0)
    added = deposit(
        row_ids,
        col_ids,
        depth_ids,
        jnp.concatenate(collected, axis=1),
        grid_rows,
        grid_cols,
        depth_bins,
        radius,
    )
    new_bias = bias_grid + added
    highest = lax.pmax(jnp.max(new_bias), ("slab", "walk"))
    free_energy = FREE_SCALE * (highest - new_bias)
    return (new_bias, free_energy)


LANES = 128
F32 = jnp.float32
BF16 = jnp.bfloat16
MESH = pl.DeviceIdType.MESH
NT = (((1,), (1,)), ((), ()))


def wrapped(offset, extent):
    offset = jnp.where(offset >= extent // 2, offset - extent, offset)
    return jnp.where(offset < -(extent // 2), offset + extent, offset)


def profile(offset, radius):
    spread = SIGMA_SHARE * radius
    value = jnp.exp(-(offset * offset) / (2.0 * spread * spread))
    return jnp.where((offset >= -radius) & (offset < radius), value, 0.0)


def halves(value):
    high = value.astype(BF16)
    return high, (value - high.astype(F32)).astype(BF16)


def iota(shape, dim):
    return lax.broadcasted_iota(jnp.int32, shape, dim).astype(F32)


def window_kernel(
    slabs, walks, rows, cols, levels, per_group,
    bias_in, slab_in, row_in, col_in, depth_in, level_in, count_in, table_in,
    new_ref, top_ref, flag_ref,
    bias_ref, slab_ref, row_ref, col_ref, depth_ref, level_ref, count_ref, table_ref, in_sems,
    mine, hills, bias_high, bias_low, own, picked, tables, chosen,
    left_high, left_low, right_high, right_low, near, peak, peaks,
    a_send, a_recv, b_send, b_recv, c_send, c_recv,
):
    devices = slabs * walks
    groups = devices // per_group
    share = LANES // per_group
    cells, depth = bias_ref.shape
    radius = 2 * rows
    grid_rows, grid_cols = slabs * rows, walks * cols
    slab = lax.axis_index("slab")
    walk = lax.axis_index("walk")
    me = slab * walks + walk
    first_row = (slab * rows).astype(F32)
    first_col = (walk * cols).astype(F32)

    def place(step):
        other = lax.rem(me + step, devices)
        return (other // walks, lax.rem(other, walks))

    steps = sorted(range(1, devices), key=lambda step: -min(step, devices - step))
    barrier = pltpu.get_barrier_semaphore()
    for step in steps:
        pl.semaphore_signal(barrier, inc=1, device_id=place(step), device_id_type=MESH)

    inputs = (
        (slab_in, slab_ref), (row_in, row_ref), (col_in, col_ref), (depth_in, depth_ref),
        (level_in, level_ref), (count_in, count_ref), (table_in, table_ref), (bias_in, bias_ref),
    )
    fetches = [
        pltpu.make_async_copy(there, here, in_sems.at[i])
        for i, (there, here) in enumerate(inputs)
    ]
    for fetch in fetches:
        fetch.start()
    for fetch in fetches[:-1]:
        fetch.wait()

    def in_row(ref):
        value = ref[...].astype(F32)
        return jnp.concatenate([value[i : i + 1] for i in range(value.shape[0])], axis=1)

    slots = row_ref.shape[1]
    lane = iota((1, LANES), 1)
    live = jnp.zeros((1, LANES), F32)
    for i in range(row_ref.shape[0]):
        inside = (lane >= i * slots) & (lane < i * slots + count_ref[i].astype(F32))
        live = jnp.where(inside, 1.0, live)
    target = in_row(slab_ref)
    centre_row = target * rows + in_row(row_ref)
    centre_col = in_row(col_ref)
    centre_depth = in_row(depth_ref)
    owner = target * walks + jnp.floor(centre_col / cols)
    owner = jnp.where(live > 0, owner, -1.0)
    owners = jnp.broadcast_to(owner, (LANES, LANES))
    same = (owners == owners.T) & (iota((LANES, LANES), 0) < iota((LANES, LANES), 1))
    rank = jnp.sum(jnp.where(same, 1.0, 0.0), axis=0, keepdims=True)
    over = jnp.max(jnp.where((live > 0) & (rank >= share), 1.0, 0.0))
    spot = rank + (lax.rem(me, per_group) * share).astype(F32)
    spot = jnp.where((live > 0) & (rank < share), spot, -1.0)
    col_high = jnp.floor(centre_col / 16.0)
    depth_high = jnp.floor(centre_depth / 16.0)
    fields = (
        jnp.where(live > 0, in_row(level_ref) + 1.0, 0.0),
        centre_row,
        col_high,
        centre_col - 16.0 * col_high,
        depth_high,
        centre_depth - 16.0 * depth_high,
        spot,
        live,
    )
    for i, field in enumerate(fields):
        mine[i : i + 1, :] = field
    hills[me] = mine[...]

    pl.semaphore_wait(barrier, devices - 1)
    a_copies = [
        pltpu.make_async_remote_copy(
            mine, hills.at[me], a_send.at[step], a_recv.at[step],
            device_id=place(step), device_id_type=MESH,
        )
        for step in steps
    ]
    for copy in a_copies:
        copy.start()

    fetches[-1].wait()
    high, low = halves(bias_ref[...])
    bias_high[...] = high
    bias_low[...] = low
    earlier = jnp.where(
        iota((LANES, LANES), 0) < iota((LANES, LANES), 1), 1.0, 0.0
    ).astype(BF16)
    one, two = (
        lax.broadcasted_iota(jnp.int32, (devices, devices), 0),
        lax.broadcasted_iota(jnp.int32, (devices, devices), 1),
    )
    before = jnp.where((one // per_group == two // per_group) & (two < one), 1.0, 0.0).astype(BF16)

    for copy in a_copies:
        copy.wait_recv()

    there = hills[:, 7, :] > 0
    hill_row = hills[:, 1, :]
    hill_col = hills[:, 2, :] * 16.0 + hills[:, 3, :]
    away_row = hill_row - first_row
    away_col = hill_col - first_col
    owned = there & (away_row >= 0) & (away_row < rows) & (away_col >= 0) & (away_col < cols)
    own_place = jnp.where(owned, hills[:, 6, :], -1.0)

    def past(away, extent, limit):
        away = away + (radius - 1)
        away = jnp.where(away < 0, away + extent, away)
        away = jnp.where(away >= extent, away - extent, away)
        return away < limit

    close = (
        there
        & past(away_row, grid_rows, rows + 2 * radius - 1)
        & past(away_col, grid_cols, cols + 2 * radius - 1)
    )
    close_one = jnp.where(close, 1.0, 0.0)
    close_half = close_one.astype(BF16)
    rank_in = jnp.dot(close_half, earlier, preferred_element_type=F32)
    rank_of = jnp.sum(
        jnp.dot(before, close_half, preferred_element_type=F32), axis=1, keepdims=True
    )
    close_place = jnp.where(close, rank_in + rank_of, -1.0)
    over = jnp.maximum(over, jnp.max(jnp.where(close_place >= LANES, 1.0, 0.0)))

    slot = iota((LANES, per_group * LANES), 0)

    def group_fields(group):
        parts = [hills[group * per_group + i] for i in range(per_group)]
        return jnp.concatenate(parts, axis=1).astype(BF16)

    def group_places(places, group):
        parts = [
            places[group * per_group + i : group * per_group + i + 1, :] for i in range(per_group)
        ]
        matches = slot == jnp.concatenate(parts, axis=1)
        return jnp.where(matches, 1.0, 0.0).astype(BF16)

    for group in range(groups):
        own[group] = lax.dot_general(
            group_fields(group), group_places(own_place, group), NT, preferred_element_type=F32
        )

    cell_id = iota((cells, 2 * LANES), 0)
    depth_id = iota((depth, 2 * LANES), 0)

    def pick(pair, carry):
        part = jnp.concatenate([own[2 * pair], own[2 * pair + 1]], axis=1)
        wanted = part[4:5] * 16.0 + part[5:6]
        select = jnp.where(depth_id == wanted, 1.0, 0.0).astype(BF16)
        lines = jnp.dot(bias_high[...], select, preferred_element_type=F32)
        lines = lines + jnp.dot(bias_low[...], select, preferred_element_type=F32)
        cell = (part[1:2] - first_row) * cols + part[2:3] * 16.0 + part[3:4] - first_col
        value = jnp.sum(jnp.where(cell_id == cell, lines, 0.0), axis=0, keepdims=True)
        picked[pl.ds(2 * pair, 1), :] = value[:, :LANES]
        picked[pl.ds(2 * pair + 1, 1), :] = value[:, LANES:]
        return carry

    lax.fori_loop(0, groups // 2, pick, 0, unroll=groups <= 8)

    offsets = [(i, j) for i in (-2, -1, 0, 1, 2) for j in (-1, 0, 1)]
    b_copies = []
    for n, (i, j) in sorted(enumerate(offsets), key=lambda item: -abs(item[1][0])):
        if (i, j) == (0, 0):
            continue
        device = (lax.rem(slab - i + slabs, slabs), lax.rem(walk - j + walks, walks))
        b_copies.append(
            pltpu.make_async_remote_copy(
                picked, tables.at[n], b_send.at[n], b_recv.at[n],
                device_id=device, device_id_type=MESH,
            )
        )
    for copy in b_copies:
        copy.start()

    depth_lane = iota((LANES, depth), 1)
    col_id = iota((cols, LANES), 0)
    for group in range(groups):
        data, places = group_fields(group), group_places(close_place, group)
        chosen[group] = lax.dot_general(data, places, NT, preferred_element_type=F32)
        column = lax.dot_general(places, data, NT, preferred_element_type=F32)
        at = column[:, 4:5] * 16.0 + column[:, 5:6]
        high, low = halves(profile(wrapped(depth_lane - at, depth), radius))
        right_high[group * LANES : (group + 1) * LANES, :] = high
        right_low[group * LANES : (group + 1) * LANES, :] = low
        part = chosen[group]
        at = part[2:3] * 16.0 + part[3:4]
        near[:, group * LANES : (group + 1) * LANES] = profile(
            wrapped(col_id + first_col - at, grid_cols), radius
        )

    level = chosen[:, 0, :]
    base = jnp.zeros((groups, LANES), F32)
    for i in range(levels):
        base = jnp.where(level == i + 1, BASE_HEIGHT * table_ref[i], base)
    at_row = chosen[:, 1, :]
    at_col = chosen[:, 2, :] * 16.0 + chosen[:, 3, :]
    at_spot = chosen[:, 6, :].astype(jnp.int32)
    slab_of = jnp.floor(at_row / rows) - slab.astype(F32)
    walk_of = jnp.floor(at_col / cols) - walk.astype(F32)
    slab_of = jnp.where(slab_of < -2, slab_of + slabs, slab_of)
    slab_of = jnp.where(slab_of > 2, slab_of - slabs, slab_of)
    walk_of = jnp.where(walk_of < -1, walk_of + walks, walk_of)
    walk_of = jnp.where(walk_of > 1, walk_of - walks, walk_of)
    row_parts = [
        profile(wrapped(first_row + r - at_row, grid_rows), radius) for r in range(rows)
    ]

    for copy in b_copies:
        copy.wait_recv()
    centre = jnp.zeros((groups, LANES), F32)
    for n, (i, j) in enumerate(offsets):
        table = picked[...] if (i, j) == (0, 0) else tables[n]
        value = jnp.take_along_axis(table, at_spot, axis=1)
        centre = jnp.where((slab_of == i) & (walk_of == j), value, centre)
    height = base * jnp.exp(-centre / TEMPER)
    row_parts = [height * part for part in row_parts]
    for r in range(rows):
        for group in range(groups):
            span = slice(group * LANES, (group + 1) * LANES)
            high, low = halves(near[:, span] * row_parts[r][group : group + 1])
            left_high[r * cols : (r + 1) * cols, span] = high
            left_low[r * cols : (r + 1) * cols, span] = low

    added = jnp.dot(left_high[...], right_high[...], preferred_element_type=F32)
    added += jnp.dot(left_low[...], right_high[...], preferred_element_type=F32)
    added += jnp.dot(left_high[...], right_low[...], preferred_element_type=F32)
    value = bias_ref[...] + added
    new_ref[...] = value
    most = jnp.max(value, axis=0, keepdims=True)
    top = most[:, 0:LANES]
    for i in range(1, depth // LANES):
        top = jnp.maximum(top, most[:, i * LANES : (i + 1) * LANES])
    top = jnp.where(over > 0, jnp.inf, top)
    peak[...] = top
    peaks[me] = top
    c_copies = [
        pltpu.make_async_remote_copy(
            peak, peaks.at[me], c_send.at[step], c_recv.at[step],
            device_id=place(step), device_id_type=MESH,
        )
        for step in steps
    ]
    for copy in c_copies:
        copy.start()
    for copy in c_copies:
        copy.wait_recv()
    highest = jnp.max(peaks[...])
    top_ref[...] = jnp.broadcast_to(highest, top_ref.shape)
    flag_ref[0] = jnp.where(highest == jnp.inf, 1, 0)
    for copy in a_copies + b_copies + c_copies:
        copy.wait_send()


def by_kernel(per_group, collective_id, slabs, walks, arrays):
    bias_grid, hill_slab, hill_row, hill_col, hill_depth, hill_level, hill_count, table = arrays
    rows, cols, depth = bias_grid.shape
    devices = slabs * walks
    groups = devices // per_group
    total = groups * LANES
    cells = rows * cols
    walkers = hill_row.shape
    vmem = pl.BlockSpec(memory_space=pltpu.VMEM)
    smem = pl.BlockSpec(memory_space=pltpu.SMEM)
    hbm = pl.BlockSpec(memory_space=pltpu.HBM)
    return pl.pallas_call(
        functools.partial(
            window_kernel, slabs, walks, rows, cols, table.shape[0], per_group
        ),
        out_shape=(
            jax.ShapeDtypeStruct((cells, depth), F32),
            jax.ShapeDtypeStruct((8, LANES), F32),
            jax.ShapeDtypeStruct((1,), jnp.int32),
        ),
        in_specs=[hbm] * 8,
        out_specs=(vmem, vmem, smem),
        scratch_shapes=[
            pltpu.VMEM((cells, depth), F32),
            pltpu.VMEM(walkers, jnp.int32),
            pltpu.VMEM(walkers, jnp.int32),
            pltpu.VMEM(walkers, jnp.int32),
            pltpu.VMEM(walkers, jnp.int32),
            pltpu.VMEM(walkers, jnp.int32),
            pltpu.SMEM(hill_count.shape, jnp.int32),
            pltpu.SMEM(table.shape, F32),
            pltpu.SemaphoreType.DMA((8,)),
            pltpu.VMEM((8, LANES), F32),
            pltpu.VMEM((devices, 8, LANES), F32),
            pltpu.VMEM((cells, depth), BF16),
            pltpu.VMEM((cells, depth), BF16),
            pltpu.VMEM((groups, 8, LANES), F32),
            pltpu.VMEM((groups, LANES), F32),
            pltpu.VMEM((15, groups, LANES), F32),
            pltpu.VMEM((groups, 8, LANES), F32),
            pltpu.VMEM((cells, total), BF16),
            pltpu.VMEM((cells, total), BF16),
            pltpu.VMEM((total, depth), BF16),
            pltpu.VMEM((total, depth), BF16),
            pltpu.VMEM((cols, total), F32),
            pltpu.VMEM((1, LANES), F32),
            pltpu.VMEM((devices, 1, LANES), F32),
            pltpu.SemaphoreType.DMA((devices,)),
            pltpu.SemaphoreType.DMA((devices,)),
            pltpu.SemaphoreType.DMA((15,)),
            pltpu.SemaphoreType.DMA((15,)),
            pltpu.SemaphoreType.DMA((devices,)),
            pltpu.SemaphoreType.DMA((devices,)),
        ],
        compiler_params=pltpu.CompilerParams(
            collective_id=collective_id,
            has_side_effects=True,
            vmem_limit_bytes=(12 + 10 * 4 // per_group) * 2**20,
        ),
    )(
        bias_grid.reshape(cells, depth),
        hill_slab.reshape(hill_row.shape),
        hill_row,
        hill_col,
        hill_depth,
        hill_level,
        hill_count,
        table,
    )


def output_kernel(new_ref, top_ref, new_out, free_out, free_ref, sems):
    parts = 4
    span = new_ref.shape[0] // parts
    first = pltpu.make_async_copy(new_ref, new_out, sems.at[0])
    first.start()
    copies = [first]
    for i in range(parts):
        rows = pl.ds(i * span, span)
        free_ref[rows, :] = FREE_SCALE * (top_ref[0:1, 0:1] - new_ref[rows, :])
        copy = pltpu.make_async_copy(free_ref.at[rows], free_out.at[rows], sems.at[1 + i])
        copy.start()
        copies.append(copy)
    for copy in copies:
        copy.wait()


def outputs(new_bias, top):
    hbm = pl.BlockSpec(memory_space=pltpu.HBM)
    return pl.pallas_call(
        output_kernel,
        out_shape=(jax.ShapeDtypeStruct(new_bias.shape, F32),) * 2,
        in_specs=[pl.BlockSpec(memory_space=pltpu.VMEM)] * 2,
        out_specs=(hbm, hbm),
        scratch_shapes=[pltpu.VMEM(new_bias.shape, F32), pltpu.SemaphoreType.DMA((5,))],
        compiler_params=pltpu.CompilerParams(vmem_limit_bytes=4 * 2**20),
    )(new_bias, top)


def per_device(*arrays):
    bias_grid = arrays[0]
    shape = bias_grid.shape
    slabs, walks = lax.axis_size("slab"), lax.axis_size("walk")
    devices = slabs * walks
    fits = (
        arrays[2].size == LANES
        and slabs >= 5
        and walks >= 3
        and devices <= 64
        and devices % 8 == 0
        and shape[1] % LANES == 0
        and shape[1] >= 2 * shape[0]
        and shape[2] % LANES == 0
        and max(walks * shape[1], shape[2]) <= 4096
        and max(slabs * shape[0], arrays[7].size) <= 255
    )
    if not fits:
        return by_collectives(*arrays)

    def finish(new_bias, top):
        new_out, free_out = outputs(new_bias, top)
        return new_out.reshape(shape), free_out.reshape(shape)

    new_bias, top, flag = by_kernel(4, 0, slabs, walks, arrays)
    return lax.cond(
        flag.reshape(()),
        lambda: finish(*by_kernel(1, 1, slabs, walks, arrays)[:2]),
        lambda: finish(new_bias, top),
    )


def solution(mesh):
    in_specs = (
        P("slab", "walk", None),
        P(("slab", "walk"), None, None),
        P(("slab", "walk"), None),
        P(("slab", "walk"), None),
        P(("slab", "walk"), None),
        P(("slab", "walk"), None),
        P(("slab", "walk")),
        P(),
    )
    out_specs = (P("slab", "walk", None), P("slab", "walk", None))
    return jax.shard_map(
        per_device, mesh=mesh, in_specs=in_specs, out_specs=out_specs, check_vma=False
    )
```
